32 devices in a mesh: rows: 16 (over z, x, core), items: 2 (over y).
Axes of the slice: x: 2, y: 2, z: 4, core: 2. Of those that a mesh axis runs over, the one named last changes fastest.
Arguments:
- frames: float32 [4, 4, 64, 64, 512], P('items', None, 'rows'), may hold values from -6 to 6
- counts: int32 [4], P('items'), may hold values from 1 to 4
- time_weight: float32 [4, 512], replicated, may hold values from 0.5 to 2
- first_gain: float32 [512], replicated, may hold values from 0.5 to 1.5
- first_shift: float32 [512], replicated, may hold values from -4 to 4
- mixing_weight: float32 [2048, 64], P(('rows', 'items')), may hold values from -0.5 to 0.5
- mixing_bias: float32 [4, 512], replicated, may hold values from -4 to 4
- second_gain: float32 [512], replicated, may hold values from 0.5 to 1.5
- second_shift: float32 [512], replicated, may hold values from -4 to 4
- expand_weight: float32 [512, 2048], P(None, ('rows', 'items')), may hold values from -0.25 to 0.25
- expand_bias: float32 [2048], replicated, may hold values from -4 to 4
- contract_weight: float32 [2048, 512], P(('rows', 'items')), may hold values from -0.125 to 0.125
- contract_bias: float32 [512], replicated, may hold values from -4 to 4
- output_cotangent: float32 [4, 64, 64, 512], P('items', 'rows'), may hold values from -6 to 6
Outputs:
- block_out: float32 [4, 64, 64, 512], P('items', 'rows')
- frames_grad: float32 [4, 4, 64, 64, 512], P('items', None, 'rows')
- time_weight_grad: float32 [4, 512], replicated
- first_gain_grad: float32 [512], replicated
- first_shift_grad: float32 [512], replicated
- mixing_weight_grad: float32 [2048, 64], P(('rows', 'items'))
- mixing_bias_grad: float32 [4, 512], replicated
- second_gain_grad: float32 [512], replicated
- second_shift_grad: float32 [512], replicated
- expand_weight_grad: float32 [512, 2048], P(None, ('rows', 'items'))
- expand_bias_grad: float32 [2048], replicated
- contract_weight_grad: float32 [2048, 512], P(('rows', 'items'))
- contract_bias_grad: float32 [512], replicated
The draws below stay inside these ranges and needn't reach their ends.
Inputs may be any that keep to these rules, and one draw needn't show every extreme that they name: counts[i] frames of item i count; the later frames are masked out.
All inputs are finite; a program needn't handle non-finite values.
Results may differ from the reference program's by a relative error of at most 0.0035.
Values sent between devices are 32-bit elements; how exact they have to be, the bound alone decides.
No kernel may reach another device: no remote copies, remote signals or barrier semaphores. Data moves between devices by JAX's collectives and lax.ppermute only.
A program may use at most 128 MiB of HBM per device.

```python
import math
import jax
import jax.numpy as jnp
from jax import lax

C = 512
F = 2048
BLOCKS = 8
MODES = 32
HG = 64
FR = 4
BS = 64
ITEMS = 4


def drawn_field(key, shape):
    values = jnp.clip(jax.random.normal(key, shape, jnp.float32), -6.0, 6.0)
    return values


def draw_frames(key, part):
    return drawn_field(jax.random.fold_in(key, 11), (ITEMS, FR, HG, HG, C))


def draw_output_cotangent(key, part):
    return drawn_field(jax.random.fold_in(key, 23), (ITEMS, HG, HG, C))


def with_ends(values, stream_key, smallest, high):
    index_at = [jax.random.randint(jax.random.fold_in(stream_key, axis), (), 0, length) for axis, length in enumerate(values.shape)]
    longest = values.shape.index(max(values.shape))
    next_to = index_at[:longest] + [(index_at[longest] + 1) % values.shape[longest]] + index_at[longest + 1:]
    return values.at[tuple(index_at)].set(smallest).at[tuple(next_to)].set(high)


def levels(rng, dims, pieces, least, high):
    level, own = 1.0, jax.random.fold_in(rng, 6)
    for dim, parts in pieces:
        steps = jnp.exp(jax.random.uniform(jax.random.fold_in(own, dim), (parts,), jnp.float32, least / len(pieces), high / len(pieces)))
        level = level * jnp.repeat(steps, dims[dim] // parts).reshape([-1 if axis == dim else 1 for axis in range(len(dims))])
    return level


def normal_values(stream_key, dims, deviation, limit, split=(), kind=jnp.bfloat16):
    loudness = levels(stream_key, dims, split, -0.22, 0.18) if split else 1.0
    values = jax.random.normal(stream_key, dims, jnp.float32) * deviation * loudness
    return jnp.minimum(jnp.maximum(values, -limit), limit).astype(kind)


def setup_inputs(seed: int = 0) -> dict:
    key_list = jax.random.split(jax.random.key(seed), 15)
    frames = draw_frames(jax.random.fold_in(key_list[14], 71), 0)
    counts = with_ends(jax.random.randint(key_list[1], (ITEMS,), 1, FR + 1), jax.random.fold_in(key_list[1], 1), 1, FR).astype(jnp.int32)
    time_weight = jnp.clip(jnp.exp(jax.random.uniform(key_list[2], (FR, C), jnp.float32, math.log(0.5), math.log(2.0))), 0.5, 2.0)
    first_gain = jnp.clip(1.0 + 0.1 * jax.random.normal(key_list[3], (C,), jnp.float32), 0.5, 1.5)
    first_shift = normal_values(key_list[4], (C,), 0.3, 4.0, (), jnp.float32)
    mixing_weight = normal_values(key_list[5], (4 * C, BS), (2 * BS) ** -0.5, 0.5, ((0, 32),), jnp.float32)
    mixing_bias = normal_values(key_list[6], (4, C), 0.3, 4.0, (), jnp.float32)
    second_gain = jnp.clip(1.0 + 0.1 * jax.random.normal(key_list[7], (C,), jnp.float32), 0.5, 1.5)
    second_shift = normal_values(key_list[8], (C,), 0.3, 4.0, (), jnp.float32)
    expand_weight = normal_values(key_list[9], (C, F), C ** -0.5, 0.25, ((1, 32),), jnp.float32)
    expand_bias = normal_values(key_list[10], (F,), 0.3, 4.0, (), jnp.float32)
    contract_weight = normal_values(key_list[11], (F, C), F ** -0.5, 0.125, ((0, 32),), jnp.float32)
    contract_bias = normal_values(key_list[12], (C,), 0.3, 4.0, (), jnp.float32)
    output_cotangent = draw_output_cotangent(jax.random.fold_in(key_list[14], 71), 0)
    return dict(frames=frames, counts=counts, time_weight=time_weight, first_gain=first_gain, first_shift=first_shift, mixing_weight=mixing_weight, mixing_bias=mixing_bias, second_gain=second_gain, second_shift=second_shift, expand_weight=expand_weight, expand_bias=expand_bias, contract_weight=contract_weight, contract_bias=contract_bias, output_cotangent=output_cotangent)


@jax.custom_vjp
def low(v):
    return lax.optimization_barrier(v.astype(jnp.bfloat16)).astype(jnp.float32)

@jax.custom_vjp
def low_back(v):
    return v

def low_keep(v):
    return (low(v), None)

def low_pass(kept, grad):
    return (grad,)

def back_keep(v):
    return (v, None)

def back_low(kept, grad):
    return (low(grad),)
low.defvjp(low_keep, low_pass)
low_back.defvjp(back_keep, back_low)
HIGHEST = lax.Precision.HIGHEST
shrink_level = 0.01
norm_eps = 1e-05

def tables():
    grid_index = jnp.arange(HG, dtype=jnp.int32)
    along_index = jnp.arange(MODES, dtype=jnp.int32)
    across_index = jnp.concatenate([jnp.arange(MODES // 2, dtype=jnp.int32), jnp.arange(HG - MODES // 2, HG, dtype=jnp.int32)])
    step_angle = 2.0 * math.pi / HG
    factor = 1.0 / math.sqrt(HG)
    width_angle = (along_index[:, None] * grid_index[None, :] % HG).astype(jnp.float32) * step_angle
    height_angle = (across_index[:, None] * grid_index[None, :] % HG).astype(jnp.float32) * step_angle
    cos_width = jnp.cos(width_angle) * factor
    sin_width = jnp.sin(width_angle) * factor
    cos_height = jnp.cos(height_angle) * factor
    sin_height = jnp.sin(height_angle) * factor
    doubled = jnp.where(along_index == 0, 1.0, 2.0).astype(jnp.float32)[:, None]
    return (cos_width, sin_width, cos_height, sin_height, cos_width * doubled, sin_width * doubled)

def layer_norm(values, norm_gain, norm_shift):
    average = lax.optimization_barrier(jnp.mean(values, axis=-1, keepdims=True))
    centred = values - average
    spread = lax.optimization_barrier(jnp.mean(centred * centred, axis=-1, keepdims=True))
    return centred * lax.rsqrt(spread + norm_eps) * norm_gain + norm_shift

def gelu_exact(values):
    return jax.nn.gelu(values, approximate=False)

def shrink(values):
    return values - jnp.clip(values, -shrink_level, shrink_level)

def mix_reference(modes_real, modes_imag, weight_table, bias_table):
    current_real, current_imag = (modes_real, modes_imag)
    for layer_index in range(2):
        weight_real = weight_table[layer_index, :, 0]
        weight_imag = weight_table[layer_index, :, 1]
        new_real = jnp.einsum('qkbi,bio->qkbo', current_real, weight_real, precision=HIGHEST) - jnp.einsum('qkbi,bio->qkbo', current_imag, weight_imag, precision=HIGHEST) + bias_table[layer_index, 0]
        new_imag = jnp.einsum('qkbi,bio->qkbo', current_imag, weight_real, precision=HIGHEST) + jnp.einsum('qkbi,bio->qkbo', current_real, weight_imag, precision=HIGHEST) + bias_table[layer_index, 1]
        if layer_index == 0:
            current_real, current_imag = (gelu_exact(new_real), gelu_exact(new_imag))
        else:
            current_real, current_imag = (shrink(new_real), shrink(new_imag))
    return (current_real, current_imag)

def forward(params, item_frames, item_count):
    time_weight, first_gain, first_shift, mixing_weight, mixing_bias, second_gain, second_shift, expand_weight, expand_bias, contract_weight, contract_bias = params
    cos_width, sin_width, cos_height, sin_height, cos_wide, sin_wide = tables()
    live = (jnp.arange(FR, dtype=jnp.int32) < item_count).astype(jnp.float32) / item_count.astype(jnp.float32)
    merged = lax.optimization_barrier(jnp.sum(item_frames * (live[:, None] * time_weight)[:, None, None, :], axis=0))
    normed = layer_norm(merged, first_gain, first_shift)
    part_real = jnp.einsum('kw,hwc->hkc', cos_width, normed, precision=HIGHEST)
    part_imag = -jnp.einsum('kw,hwc->hkc', sin_width, normed, precision=HIGHEST)
    modes_real = jnp.einsum('qh,hkc->qkc', cos_height, part_real, precision=HIGHEST) + jnp.einsum('qh,hkc->qkc', sin_height, part_imag, precision=HIGHEST)
    modes_imag = jnp.einsum('qh,hkc->qkc', cos_height, part_imag, precision=HIGHEST) - jnp.einsum('qh,hkc->qkc', sin_height, part_real, precision=HIGHEST)
    weight_table = mixing_weight.reshape(2, BLOCKS, 2, BS, BS)
    bias_table = mixing_bias.reshape(2, 2, BLOCKS, BS)
    mixed_real, mixed_imag = mix_reference(modes_real.reshape(MODES, MODES, BLOCKS, BS), modes_imag.reshape(MODES, MODES, BLOCKS, BS), weight_table, bias_table)
    mixed_real = mixed_real.reshape(MODES, MODES, C)
    mixed_imag = mixed_imag.reshape(MODES, MODES, C)
    back_real = jnp.einsum('qh,qkc->hkc', cos_height, mixed_real, precision=HIGHEST) - jnp.einsum('qh,qkc->hkc', sin_height, mixed_imag, precision=HIGHEST)
    back_imag = jnp.einsum('qh,qkc->hkc', cos_height, mixed_imag, precision=HIGHEST) + jnp.einsum('qh,qkc->hkc', sin_height, mixed_real, precision=HIGHEST)
    spatial = jnp.einsum('kw,hkc->hwc', cos_wide, back_real, precision=HIGHEST) - jnp.einsum('kw,hkc->hwc', sin_wide, back_imag, precision=HIGHEST)
    middle = merged + spatial
    normed_two = layer_norm(middle, second_gain, second_shift)
    hidden = gelu_exact(jnp.dot(normed_two.reshape(HG * HG, C), expand_weight, precision=HIGHEST) + expand_bias)
    update = jnp.dot(hidden, contract_weight, precision=HIGHEST) + contract_bias
    return middle + update.reshape(HG, HG, C)

def add_pair(first_term, second_term):
    return first_term + second_term

def reference(frames, counts, time_weight, first_gain, first_shift, mixing_weight, mixing_bias, second_gain, second_shift, expand_weight, expand_bias, contract_weight, contract_bias, output_cotangent):
    params = (time_weight, first_gain, first_shift, mixing_weight, mixing_bias, second_gain, second_shift, expand_weight, expand_bias, contract_weight, contract_bias)

    def one_item(totals, inputs):
        item_frames, item_count, item_cotangent = inputs

        def local_forward(params_in, frames_in):
            return forward(params_in, frames_in, item_count)
        result, pullback = jax.vjp(local_forward, params, item_frames)
        param_grads, frame_grads = pullback(item_cotangent)
        totals = jax.tree.map(add_pair, totals, param_grads)
        return (totals, (result, frame_grads))
    zeros = jax.tree.map(jnp.zeros_like, params)
    totals, outputs = lax.scan(one_item, zeros, (frames, counts, output_cotangent))
    results, frame_grads = outputs
    return (results, frame_grads, totals[0], totals[1], totals[2], totals[3], totals[4], totals[5], totals[6], totals[7], totals[8], totals[9], totals[10])
```

```python
import math

import jax
import jax.numpy as jnp
import numpy as np
from jax import lax
from jax.experimental import pallas as pl
from jax.experimental.pallas import tpu as pltpu
from jax.sharding import PartitionSpec as P

BLOCKS = 8
MODES = 32
PAIRS = BLOCKS // 2
HIGHEST = lax.Precision.HIGHEST
SHRINK = 0.01
EPS = 1e-05
F32 = jnp.float32
BF16 = jnp.bfloat16
AXES = ("rows", "items")
LIMIT = 56 * 1024 * 1024
HALF_ROOT = math.sqrt(0.5)
DENSITY = 1.0 / math.sqrt(2.0 * math.pi)


def make_tables(grid_size, rows_local, row_parts):
    n = np.arange(grid_size)
    along = np.arange(MODES)
    across = np.concatenate(
        [np.arange(MODES // 2), np.arange(grid_size - MODES // 2, grid_size)]
    )
    step = 2.0 * np.pi / grid_size
    factor = 1.0 / np.sqrt(grid_size)
    wide = (along[:, None] * n[None, :] % grid_size) * step
    high = (across[:, None] * n[None, :] % grid_size) * step
    cos_w, sin_w = np.cos(wide) * factor, np.sin(wide) * factor
    cos_h, sin_h = np.cos(high) * factor, np.sin(high) * factor
    doubled = np.where(along == 0, 1.0, 2.0)[:, None]
    eye = np.eye(rows_local)
    forward = np.einsum("pkw,hg->kphgw", np.stack([cos_w, -sin_w]), eye)
    forward = forward.reshape(MODES * 2 * rows_local, rows_local * grid_size)
    inverse = np.einsum("pkw,hg->gwkph", np.stack([cos_w * doubled, -sin_w * doubled]), eye)
    inverse = inverse.reshape(rows_local * grid_size, MODES * 2 * rows_local)
    column = np.stack([np.stack([cos_h, sin_h]), np.stack([-sin_h, cos_h])])
    column = column.reshape(2, 2, MODES, row_parts, rows_local)
    column = column.transpose(0, 2, 3, 1, 4).reshape(2 * MODES, row_parts * 2 * rows_local)
    as32 = lambda x: np.ascontiguousarray(x, dtype=np.float32)
    return (
        as32(forward),
        as32(forward.T),
        as32(inverse),
        as32(inverse.T),
        as32(column),
        as32(column.T),
    )


def dot_full(a, b):
    return jnp.dot(a, b, precision=HIGHEST, preferred_element_type=F32)


def halves(x):
    high = x.astype(BF16)
    return high, (x - high.astype(F32)).astype(BF16)


def dot_pairs(a, b, dims):
    spec = (dims, ((), ()))
    one = lambda x, y: lax.dot_general(x, y, spec, preferred_element_type=F32)
    return one(a[0], b[0]) + (one(a[0], b[1]) + one(a[1], b[0]))


NN = ((1,), (0,))
NT = ((1,), (1,))
TN = ((0,), (0,))


def cdf(v):
    return 0.5 + 0.5 * lax.erf(v * HALF_ROOT)


def density(v):
    return DENSITY * jnp.exp(-0.5 * v * v)


def normalise(v):
    average = jnp.mean(v, axis=-1, keepdims=True)
    centred = v - average
    spread = jnp.mean(centred * centred, axis=-1, keepdims=True)
    scale = lax.rsqrt(spread + EPS)
    return centred * scale, scale


def normal_back(unit, scale, weighted):
    m0 = jnp.mean(weighted, axis=-1, keepdims=True)
    m1 = jnp.mean(weighted * unit, axis=-1, keepdims=True)
    return scale * (weighted - m0 - unit * m1)


def call(body, grid, in_specs, out_specs, out_shape, flops, moved, name, scratch=()):
    return pl.pallas_call(
        body,
        grid=grid,
        in_specs=in_specs,
        out_specs=out_specs,
        out_shape=out_shape,
        scratch_shapes=list(scratch),
        name=name,
        cost_estimate=pl.CostEstimate(
            flops=int(flops), transcendentals=0, bytes_accessed=int(moved)
        ),
        compiler_params=pltpu.CompilerParams(vmem_limit_bytes=LIMIT),
    )


def whole(shape):
    return pl.BlockSpec(shape, lambda *_: (0,) * len(shape))


def build(row_parts, item_parts):
    row_bits = row_parts.bit_length() - 1
    item_bits = item_parts.bit_length() - 1
    device_total = row_parts * item_parts
    lanes = 128

    def flip(x, bit):
        pairs = [(f, f ^ (1 << bit)) for f in range(device_total)]
        return lax.ppermute(x, AXES, pairs)

    core_bit = item_bits
    depth_bits = [item_bits + row_bits - 1, item_bits + row_bits - 2]
    plane_a = [item_bits + b for b in range(row_bits - 3, 0, -1)] + list(range(item_bits))
    plane_b = plane_a[::-1]
    plane_count = len(plane_a)
    all_bits = [core_bit] + plane_a + depth_bits[::-1]
    low_bits = row_bits - 3 + item_bits
    mixing_bits = list(range(low_bits)) + [item_bits + row_bits - 1]

    def gather_stages(x, bits):
        for bit in bits:
            x = jnp.concatenate([x, flip(x, bit)], axis=0)
        return x

    def scatter_stages(x, bits):
        for bit in bits[::-1]:
            half = x.shape[0] // 2
            x = x[:half] + flip(x[half:], bit)
        return x

    def xor_order(x, index):
        for bit in range(x.shape[0].bit_length() - 1):
            lead = x.reshape((-1, 2, 1 << bit) + x.shape[1:])
            swapped = (index >> bit) % 2 == 1
            x = jnp.where(swapped, lead[:, ::-1], lead).reshape(x.shape)
        return x

    def turn_plane(x):
        lead = x.reshape((2,) * plane_count + (-1, x.shape[-1]))
        order = tuple(range(plane_count))[::-1] + (plane_count, plane_count + 1)
        return lead.transpose(order).reshape(x.shape)

    def total(x):
        for bit in all_bits:
            x = x + flip(x, bit)
        return x

    def local(
        frames,
        counts,
        time_weight,
        first_gain,
        first_shift,
        mixing_weight,
        mixing_bias,
        second_gain,
        second_shift,
        expand_weight,
        expand_bias,
        contract_weight,
        contract_bias,
        output_cotangent,
    ):
        items, frame_total, rows_local, width, channels = frames.shape
        grid_size = rows_local * row_parts
        tokens = rows_local * width
        wave_rows = MODES * 2 * rows_local
        groups = row_parts // PAIRS
        kept = MODES // groups
        part = kept * 2 * rows_local
        stack = 2 * rows_local
        mode_rows = kept * MODES
        shard = contract_weight.shape[0]
        hidden_total = expand_bias.shape[0]
        hidden_local = hidden_total // 2
        aligned = stack % 8 == 0
        tables = make_tables(grid_size, rows_local, row_parts)
        wave_fwd, wave_fwd_t, wave_inv, wave_inv_t, col, col_t = tables

        row_index = lax.axis_index("rows")
        flat = row_index * item_parts + lax.axis_index("items")
        core = row_index % 2
        pair = (row_index // (row_parts // 8)) % PAIRS
        top = row_index // (row_parts // 2)
        mixing_index = top * (1 << low_bits) + flat % (1 << low_bits)
        mixing_count = 2 << low_bits

        both = jnp.concatenate([expand_weight.T, contract_weight], axis=0)
        both = both.reshape(2, shard, channels).transpose(1, 0, 2).reshape(shard, 2 * channels)
        deep = gather_stages(both, depth_bits)
        expand_rows = gather_stages(deep[:, :channels], plane_a)
        contract_rows = turn_plane(gather_stages(deep[:, channels:], plane_b))

        pieces = gather_stages(mixing_weight.reshape(1, -1, lanes), mixing_bits)
        block_size = channels // BLOCKS
        layers = xor_order(pieces, mixing_index).reshape(2, 2, 2, block_size, block_size)

        def blocks_of(w):
            zero = jnp.zeros_like(w[0])
            return jnp.concatenate(
                [jnp.concatenate([w[0], zero], 1), jnp.concatenate([zero, w[1]], 1)], 0
            )

        def big(w):
            real, imag = blocks_of(w[:, 0]), blocks_of(w[:, 1])
            return jnp.concatenate(
                [jnp.concatenate([real, imag], 1), jnp.concatenate([-imag, real], 1)], 0
            )

        mix_weight = jnp.stack([big(layers[0]), big(layers[1])])
        bias_pairs = mixing_bias.reshape(2, 2, PAIRS, lanes)
        mix_bias = lax.dynamic_index_in_dim(bias_pairs, pair, 2, keepdims=False)
        mix_bias = mix_bias.reshape(2, 1, 2 * lanes)

        masks = [0]
        for bit in depth_bits + plane_a:
            masks = masks + [m | (1 << bit) for m in masks]
        owners = flat ^ jnp.array(masks, dtype=jnp.int32)
        pick = (
            owners[:, None] == jnp.arange(device_total, dtype=jnp.int32)[None, :]
        ).astype(F32)
        bias_shards = expand_bias.reshape(device_total, shard)
        bias_local = jnp.dot(pick, bias_shards, precision=HIGHEST).reshape(1, hidden_local)

        counts_f = counts.astype(F32)
        live = jnp.arange(frame_total, dtype=jnp.int32)[None, :] < counts[:, None]
        live = live.astype(F32) / counts_f[:, None]
        factor = live[:, :, None] * time_weight[None]
        live_wide = jnp.broadcast_to(live[:, :, None], factor.shape)
        first_pair = jnp.stack([first_gain, first_shift])
        second_pair = jnp.stack([second_gain, second_shift])

        send_shape = (2, PAIRS, groups // 2, items, part, lanes)

        def put_parts(ref, values):
            if not aligned:
                ref[0] = values
                return
            for g in range(groups):
                for p in range(PAIRS):
                    ref[g // (groups // 2), p, g % (groups // 2), 0] = values[
                        g * part : (g + 1) * part, p * lanes : (p + 1) * lanes
                    ]

        def get_parts(ref):
            if not aligned:
                return ref[0]
            rows = []
            for g in range(groups):
                rows.append(
                    jnp.concatenate(
                        [
                            ref[g // (groups // 2), p, g % (groups // 2), 0]
                            for p in range(PAIRS)
                        ],
                        axis=1,
                    )
                )
            return jnp.concatenate(rows, axis=0)

        natural = (items, wave_rows, channels)
        parts_type = jax.ShapeDtypeStruct(send_shape if aligned else natural, F32)
        if aligned:
            parts_spec = pl.BlockSpec(
                (2, PAIRS, groups // 2, 1, part, lanes), lambda i: (0, 0, 0, i, 0, 0)
            )
        else:
            parts_spec = pl.BlockSpec((1, wave_rows, channels), lambda i: (i, 0, 0))

        def to_send(x):
            if aligned:
                return x
            x = x.reshape(items, 2, groups // 2, part, PAIRS, lanes)
            return x.transpose(1, 4, 2, 0, 3, 5)

        def from_send(x):
            x = x.reshape(send_shape)
            if aligned:
                return x
            return x.transpose(3, 0, 2, 4, 1, 5).reshape(natural)

        def exchange(x):
            return lax.all_to_all(x.reshape(row_parts, -1, lanes), "rows", 0, 0)

        source_shape = (row_parts, items, kept, stack, lanes)
        turned = (items, kept, row_parts * stack, lanes)
        column_type = jax.ShapeDtypeStruct(source_shape if aligned else turned, F32)
        if aligned:
            column_spec = pl.BlockSpec(
                (row_parts, 1, kept, stack, lanes), lambda i: (0, i, 0, 0, 0)
            )
        else:
            column_spec = pl.BlockSpec((1,) + turned[1:], lambda i: (i, 0, 0, 0))

        def to_columns(x):
            x = x.reshape(source_shape)
            if aligned:
                return x
            return x.transpose(1, 2, 0, 3, 4).reshape(turned)

        def from_columns(x):
            if aligned:
                return x
            x = x.reshape(items, kept, row_parts, stack, lanes)
            return x.transpose(2, 0, 1, 3, 4)

        def get_columns(ref):
            if aligned:
                pieces = [ref[:, 0, k].reshape(row_parts * stack, lanes) for k in range(kept)]
            else:
                pieces = [ref[0, k] for k in range(kept)]
            return jnp.concatenate(pieces, axis=1)

        def put_columns(ref, values):
            for k in range(kept):
                piece = values[:, k * lanes : (k + 1) * lanes]
                if aligned:
                    ref[:, 0, k] = piece.reshape(row_parts, stack, lanes)
                else:
                    ref[0, k] = piece

        def modes_rows(m):
            return jnp.concatenate(
                [
                    jnp.concatenate(
                        [
                            m[:MODES, k * lanes : (k + 1) * lanes],
                            m[MODES:, k * lanes : (k + 1) * lanes],
                        ],
                        axis=1,
                    )
                    for k in range(kept)
                ],
                axis=0,
            )

        def rows_modes(z):
            return jnp.concatenate(
                [
                    jnp.concatenate(
                        [
                            z[k * MODES : (k + 1) * MODES, :lanes],
                            z[k * MODES : (k + 1) * MODES, lanes:],
                        ],
                        axis=0,
                    )
                    for k in range(kept)
                ],
                axis=1,
            )

        item_spec = pl.BlockSpec((1, tokens, channels), lambda i: (i, 0, 0))
        item_type = jax.ShapeDtypeStruct((items, tokens, channels), F32)
        frames_spec = pl.BlockSpec(
            (1, frame_total, rows_local, width, channels), lambda i: (i, 0, 0, 0, 0)
        )
        factor_spec = pl.BlockSpec((1, frame_total, channels), lambda i: (i, 0, 0))
        wave_spec = whole((wave_rows, tokens))
        wave_spec_t = whole((tokens, wave_rows))
        pair_spec = whole((2, channels))
        item_bytes = items * tokens * channels * 4
        wave_flops = 2 * 6 * items * wave_rows * tokens * channels

        def head_body(frames_ref, factor_ref, pair_ref, table_ref, merged_ref, parts_ref):
            merged = 0.0
            for f in range(frame_total):
                frame = frames_ref[0, f].reshape(tokens, channels)
                merged = merged + frame * factor_ref[0, f : f + 1, :]
            merged_ref[0] = merged
            unit, _ = normalise(merged)
            normed = unit * pair_ref[0:1, :] + pair_ref[1:2, :]
            put_parts(parts_ref, dot_full(table_ref[...], normed))

        merged, head_parts = call(
            head_body,
            (items,),
            [frames_spec, factor_spec, pair_spec, wave_spec],
            [item_spec, parts_spec],
            [item_type, parts_type],
            wave_flops,
            item_bytes * (frame_total + 2),
            "head",
        )(frames, factor, first_pair, wave_fwd)
        columns = to_columns(exchange(to_send(head_parts)))

        mode_spec = pl.BlockSpec((1, mode_rows, 2 * lanes), lambda i: (i, 0, 0))
        mode_type = jax.ShapeDtypeStruct((items, mode_rows, 2 * lanes), F32)
        weight_spec = whole((2, 2 * lanes, 2 * lanes))
        bias_spec = whole((2, 1, 2 * lanes))
        col_spec = whole(col.shape)
        col_spec_t = whole(col_t.shape)
        mix_flops = 2 * 6 * items * (2 * mode_rows * 4 * lanes * lanes + 2 * 64 * 128 * kept * lanes)

        def mix_body(x_ref, w_ref, b_ref, col_ref, col_t_ref, out_ref, z_ref, u_ref, v_ref):
            z = modes_rows(dot_full(col_ref[...], get_columns(x_ref)))
            z_ref[0] = z
            u = dot_full(z, w_ref[0]) + b_ref[0]
            u_ref[0] = u
            v = dot_full(u * cdf(u), w_ref[1]) + b_ref[1]
            v_ref[0] = v
            mixed = v - jnp.clip(v, -SHRINK, SHRINK)
            put_columns(out_ref, dot_full(col_t_ref[...], rows_modes(mixed)))

        back, modes_in, first_pre, second_pre = call(
            mix_body,
            (items,),
            [column_spec, weight_spec, bias_spec, col_spec, col_spec_t],
            [column_spec, mode_spec, mode_spec, mode_spec],
            [column_type, mode_type, mode_type, mode_type],
            mix_flops,
            item_bytes * 4,
            "mix",
        )(columns, mix_weight, mix_bias, col, col_t)
        row_back = from_send(exchange(from_columns(back)))

        def split_body(a_ref, b_ref, ah, al, bh, bl):
            ah[...], al[...] = halves(a_ref[...])
            bh[...], bl[...] = halves(b_ref[...])

        split_rows = hidden_local // 4
        split_spec = pl.BlockSpec((split_rows, channels), lambda i: (i, 0))
        half_type = jax.ShapeDtypeStruct((hidden_local, channels), BF16)
        up_h, up_l, down_h, down_l = call(
            split_body,
            (4,),
            [split_spec] * 2,
            [split_spec] * 4,
            [half_type] * 4,
            0,
            hidden_local * channels * 16,
            "split_weights",
        )(expand_rows, contract_rows)

        token_total = items * tokens
        cot_own = output_cotangent.reshape(token_total, channels)
        cot_other = flip(cot_own, core_bit)

        block = min(256, token_total)
        token_spec = pl.BlockSpec((block, channels), lambda i: (i, 0))
        wide_spec = pl.BlockSpec((block, hidden_local), lambda i: (i, 0))
        weight_all = whole((hidden_local, channels))
        ff_flops = 2 * 3 * token_total * channels * hidden_local

        def cot_body(g_ref, dh_ref, dl_ref, gh_ref, hi_ref, lo_ref):
            g = halves(g_ref[...])
            hi_ref[...], lo_ref[...] = g
            gh_ref[...] = dot_pairs(g, (dh_ref[...], dl_ref[...]), NT)

        def cot_call(g):
            return call(
                cot_body,
                (token_total // block,),
                [token_spec, weight_all, weight_all],
                [wide_spec, token_spec, token_spec],
                [
                    jax.ShapeDtypeStruct((token_total, hidden_local), F32),
                    jax.ShapeDtypeStruct((token_total, channels), BF16),
                    jax.ShapeDtypeStruct((token_total, channels), BF16),
                ],
                ff_flops,
                token_total * (hidden_local + channels * 2) * 4,
                "cotangent_up",
            )(g, down_h, down_l)

        gh_own, gh_own_h, gh_own_l = cot_call(cot_own)
        gh_other, gh_other_h, gh_other_l = cot_call(cot_other)

        def spatial_body(parts_ref, merged_ref, pair_ref, table_ref, middle_ref, normed_ref):
            middle = merged_ref[0] + dot_full(table_ref[...], get_parts(parts_ref))
            middle_ref[0] = middle
            unit, _ = normalise(middle)
            normed_ref[0] = unit * pair_ref[0:1, :] + pair_ref[1:2, :]

        middle, normed_two = call(
            spatial_body,
            (items,),
            [parts_spec, item_spec, pair_spec, wave_spec_t],
            [item_spec, item_spec],
            [item_type, item_type],
            wave_flops,
            item_bytes * 4,
            "spatial",
        )(row_back, merged, second_pair, wave_inv)

        pieces_total = 4
        chunk = hidden_local // pieces_total

        def feed_body(n_ref, gh_ref, uh_ref, ul_ref, bias_ref, hh, hl, ph, pl_, grad_ref, bg_ref, nh, nl):
            n = halves(n_ref[...])
            nh[...], nl[...] = n
            grad = 0.0

            @pl.when(pl.program_id(0) == 0)
            def _():
                bg_ref[...] = jnp.zeros_like(bg_ref)

            for q in range(pieces_total):
                cut = slice(q * chunk, (q + 1) * chunk)
                w = (uh_ref[cut, :], ul_ref[cut, :])
                pre = dot_pairs(n, w, NT) + bias_ref[:, cut]
                phi = cdf(pre)
                hh[:, cut], hl[:, cut] = halves(pre * phi)
                gp = gh_ref[:, cut] * (phi + pre * density(pre))
                bg_ref[:, cut] += jnp.sum(gp, axis=0, keepdims=True)
                gp = halves(gp)
                ph[:, cut], pl_[:, cut] = gp
                grad = grad + dot_pairs(gp, w, NN)
            grad_ref[...] = grad

        def feed_call(n, gh):
            wide_half = jax.ShapeDtypeStruct((token_total, hidden_local), BF16)
            slim_half = jax.ShapeDtypeStruct((token_total, channels), BF16)
            return call(
                feed_body,
                (token_total // block,),
                [token_spec, wide_spec, weight_all, weight_all, whole((1, hidden_local))],
                [wide_spec] * 4
                + [token_spec, whole((1, hidden_local)), token_spec, token_spec],
                [wide_half] * 4
                + [
                    jax.ShapeDtypeStruct((token_total, channels), F32),
                    jax.ShapeDtypeStruct((1, hidden_local), F32),
                    slim_half,
                    slim_half,
                ],
                2 * ff_flops,
                token_total * (hidden_local * 3 + channels * 3) * 4,
                "feed_forward",
            )(n, gh, up_h, up_l, bias_local)

        normed_own = normed_two.reshape(token_total, channels)
        normed_other = flip(normed_own, core_bit)
        own = feed_call(normed_own, gh_own)
        other = feed_call(normed_other, gh_other)
        grad_own = own[4]
        grad_back = flip(other[4], core_bit)
        bias_grad_local = own[5] + other[5]

        def middle_body(
            mid_ref, g1_ref, g2_ref, cot_ref, pair_ref, table_ref, gm_ref, parts_ref, small_ref
        ):
            unit, scale = normalise(mid_ref[0])
            grad = g1_ref[0] + g2_ref[0]
            cot = cot_ref[0]
            gm = cot + normal_back(unit, scale, grad * pair_ref[0:1, :])
            gm_ref[0] = gm
            put_parts(parts_ref, dot_full(table_ref[...], gm))

            @pl.when(pl.program_id(0) == 0)
            def _():
                small_ref[...] = jnp.zeros_like(small_ref)

            small_ref[0:1, :] += jnp.sum(grad * unit, axis=0, keepdims=True)
            small_ref[1:2, :] += jnp.sum(grad, axis=0, keepdims=True)
            small_ref[2:3, :] += jnp.sum(cot, axis=0, keepdims=True)

        as_items = lambda x: x.reshape(items, tokens, channels)
        small_type = jax.ShapeDtypeStruct((8, channels), F32)
        small_spec = whole((8, channels))
        grad_middle, middle_parts, small_two = call(
            middle_body,
            (items,),
            [item_spec] * 4 + [pair_spec, wave_spec],
            [item_spec, parts_spec, small_spec],
            [item_type, parts_type, small_type],
            wave_flops,
            item_bytes * 6,
            "middle_back",
        )(
            middle,
            as_items(grad_own),
            as_items(grad_back),
            as_items(cot_own),
            second_pair,
            wave_inv_t,
        )
        grad_columns = to_columns(exchange(to_send(middle_parts)))

        def down_body(hh, hl, dh, dl, out_ref):
            out_ref[...] = dot_pairs((hh[...], hl[...]), (dh[...], dl[...]), NN)

        def down_call(h):
            return call(
                down_body,
                (token_total // block,),
                [wide_spec, wide_spec, weight_all, weight_all],
                token_spec,
                jax.ShapeDtypeStruct((token_total, channels), F32),
                ff_flops,
                token_total * (hidden_local + channels) * 4,
                "contract",
            )(h[0], h[1], down_h, down_l)

        update_own = down_call(own)
        update_back = flip(down_call(other), core_bit)
        block_out = (
            middle.reshape(token_total, channels) + update_own + update_back + contract_bias[None]
        )

        piece_spec = pl.BlockSpec((token_total, chunk), lambda q: (0, q))
        slim_spec = whole((token_total, channels))
        grad_spec = pl.BlockSpec((chunk, channels), lambda q: (q, 0))

        def outer_body(a1h, a1l, a2h, a2l, b1h, b1l, b2h, b2l, out_ref):
            out_ref[...] = dot_pairs(
                (a1h[...], a1l[...]), (b1h[...], b1l[...]), TN
            ) + dot_pairs((a2h[...], a2l[...]), (b2h[...], b2l[...]), TN)

        def outer_call(a, b, name):
            return call(
                outer_body,
                (pieces_total,),
                [piece_spec] * 4 + [slim_spec] * 4,
                grad_spec,
                jax.ShapeDtypeStruct((hidden_local, channels), F32),
                2 * ff_flops,
                (token_total * (hidden_local + channels) * 2 + hidden_local * channels) * 4,
                name,
            )(*a, *b)

        contract_grad = outer_call(
            (own[0], own[1], other[0], other[1]),
            (gh_own_h, gh_own_l, gh_other_h, gh_other_l),
            "contract_grad",
        )
        expand_grad = outer_call(
            (own[2], own[3], other[2], other[3]),
            (own[6], own[7], other[6], other[7]),
            "expand_grad",
        )
        expand_part = scatter_stages(expand_grad, plane_a)
        contract_part = scatter_stages(turn_plane(contract_grad), plane_b)
        both_grad = scatter_stages(
            jnp.concatenate([expand_part, contract_part], axis=1), depth_bits
        )
        expand_weight_grad = both_grad[:, :channels].T
        contract_weight_grad = both_grad[:, channels:]

        def mix_back_body(
            x_ref, z_ref, u_ref, v_ref, w_ref, col_ref, col_t_ref, out_ref, wg_ref, bg_ref
        ):
            @pl.when(pl.program_id(0) == 0)
            def _():
                wg_ref[...] = jnp.zeros_like(wg_ref)
                bg_ref[...] = jnp.zeros_like(bg_ref)

            grad = modes_rows(dot_full(col_ref[...], get_columns(x_ref)))
            e1 = jnp.where(jnp.abs(v_ref[0]) > SHRINK, grad, 0.0)
            u = u_ref[0]
            phi = cdf(u)
            spec = lambda dims: (dims, ((), ()))
            full = lambda a, b, dims: lax.dot_general(
                a, b, spec(dims), precision=HIGHEST, preferred_element_type=F32
            )
            e0 = full(e1, w_ref[1], NT) * (phi + u * density(u))
            wg_ref[0] += full(z_ref[0], e0, TN)
            wg_ref[1] += full(u * phi, e1, TN)
            bg_ref[0] += jnp.sum(e0, axis=0, keepdims=True)
            bg_ref[1] += jnp.sum(e1, axis=0, keepdims=True)
            dz = full(e0, w_ref[0], NT)
            put_columns(out_ref, dot_full(col_t_ref[...], rows_modes(dz)))

        grad_back_parts, big_grad, big_bias = call(
            mix_back_body,
            (items,),
            [column_spec, mode_spec, mode_spec, mode_spec, weight_spec, col_spec, col_spec_t],
            [column_spec, weight_spec, bias_spec],
            [
                column_type,
                jax.ShapeDtypeStruct((2, 2 * lanes, 2 * lanes), F32),
                jax.ShapeDtypeStruct((2, 1, 2 * lanes), F32),
            ],
            2 * mix_flops,
            item_bytes * 4,
            "mix_back",
        )(grad_columns, modes_in, first_pre, second_pre, mix_weight, col, col_t)
        last_parts = from_send(exchange(from_columns(grad_back_parts)))

        def unblock(w):
            rr, ri = w[:lanes, :lanes], w[:lanes, lanes:]
            ir, ii = w[lanes:, :lanes], w[lanes:, lanes:]
            real, imag = rr + ii, ri - ir
            cut = lambda m, b: m[
                b * block_size : (b + 1) * block_size, b * block_size : (b + 1) * block_size
            ]
            return jnp.stack([jnp.stack([cut(real, b), cut(imag, b)]) for b in range(2)])

        mix_grad = jnp.stack([unblock(big_grad[0]), unblock(big_grad[1])])
        mix_grad = mix_grad.reshape(mixing_count, -1, lanes)
        mix_grad = xor_order(mix_grad, mixing_index)
        mixing_weight_grad = scatter_stages(mix_grad, mixing_bits).reshape(mixing_weight.shape)

        bias_full = jnp.zeros((2, 2, PAIRS, lanes), F32)
        bias_full = lax.dynamic_update_slice(
            bias_full, big_bias.reshape(2, 2, 1, lanes), (0, 0, pair, 0)
        ).reshape(4, channels)
        hidden_bias = jnp.dot(
            pick.T, bias_grad_local.reshape(-1, shard), precision=HIGHEST
        ).reshape(-1, channels)
        early = total(jnp.concatenate([small_two[:3], bias_full, hidden_bias], axis=0))

        def final_body(
            parts_ref,
            merged_ref,
            gm_ref,
            frames_ref,
            factor_ref,
            live_ref,
            pair_ref,
            table_ref,
            out_ref,
            small_ref,
        ):
            grad = dot_full(table_ref[...], get_parts(parts_ref))
            unit, scale = normalise(merged_ref[0])
            gm = gm_ref[0] + normal_back(unit, scale, grad * pair_ref[0:1, :])

            @pl.when(pl.program_id(0) == 0)
            def _():
                small_ref[...] = jnp.zeros_like(small_ref)

            small_ref[frame_total : frame_total + 1, :] += jnp.sum(
                grad * unit, axis=0, keepdims=True
            )
            small_ref[frame_total + 1 : frame_total + 2, :] += jnp.sum(
                grad, axis=0, keepdims=True
            )
            for f in range(frame_total):
                frame = frames_ref[0, f].reshape(tokens, channels)
                small_ref[f : f + 1, :] += live_ref[0, f : f + 1, :] * jnp.sum(
                    frame * gm, axis=0, keepdims=True
                )
                out_ref[0, f] = (gm * factor_ref[0, f : f + 1, :]).reshape(
                    rows_local, width, channels
                )

        frames_grad, small_one = call(
            final_body,
            (items,),
            [parts_spec, item_spec, item_spec, frames_spec, factor_spec, factor_spec]
            + [pair_spec, wave_spec_t],
            [frames_spec, small_spec],
            [jax.ShapeDtypeStruct(frames.shape, F32), small_type],
            wave_flops,
            item_bytes * (3 + 2 * frame_total),
            "final",
        )(last_parts, merged, grad_middle, frames, factor, live_wide, first_pair, wave_fwd_t)
        late = total(small_one[: frame_total + 2])

        return (
            block_out.reshape(output_cotangent.shape),
            frames_grad,
            late[:frame_total],
            late[frame_total],
            late[frame_total + 1],
            mixing_weight_grad,
            early[3:7],
            early[0],
            early[1],
            expand_weight_grad,
            early[7:].reshape(hidden_total),
            contract_weight_grad,
            early[2],
        )

    return local


def solution(mesh):
    return jax.shard_map(
        build(mesh.shape["rows"], mesh.shape["items"]),
        mesh=mesh,
        in_specs=(
            P("items", None, "rows", None, None),
            P("items"),
            P(),
            P(),
            P(),
            P(("rows", "items"), None),
            P(),
            P(),
            P(),
            P(None, ("rows", "items")),
            P(),
            P(("rows", "items"), None),
            P(),
            P("items", "rows", None, None),
        ),
        out_specs=(
            P("items", "rows", None, None),
            P("items", None, "rows", None, None),
            P(),
            P(),
            P(),
            P(("rows", "items"), None),
            P(),
            P(),
            P(),
            P(None, ("rows", "items")),
            P(),
            P(("rows", "items"), None),
            P(),
        ),
        check_vma=False,
    )
```

```python
import math

import jax
import jax.numpy as jnp
import numpy as np
from jax import lax
from jax.experimental import pallas as pl
from jax.experimental.pallas import tpu as pltpu
from jax.sharding import PartitionSpec as P

BLOCKS = 8
MODES = 32
PAIRS = BLOCKS // 2
HIGHEST = lax.Precision.HIGHEST
SHRINK = 0.01
EPS = 1e-05
F32 = jnp.float32
BF16 = jnp.bfloat16
PLANNED = 0.001
AXES = ("rows", "items")
LIMIT = 56 * 1024 * 1024
HALF_ROOT = math.sqrt(0.5)
DENSITY = 1.0 / math.sqrt(2.0 * math.pi)


def after(x, *others):
    return lax.optimization_barrier((x,) + others)[0]


def make_tables(grid_size, rows_local, row_parts):
    n = np.arange(grid_size)
    along = np.arange(MODES)
    across = np.concatenate(
        [np.arange(MODES // 2), np.arange(grid_size - MODES // 2, grid_size)]
    )
    step = 2.0 * np.pi / grid_size
    factor = 1.0 / np.sqrt(grid_size)
    wide = (along[:, None] * n[None, :] % grid_size) * step
    high = (across[:, None] * n[None, :] % grid_size) * step
    cos_w, sin_w = np.cos(wide) * factor, np.sin(wide) * factor
    cos_h, sin_h = np.cos(high) * factor, np.sin(high) * factor
    doubled = np.where(along == 0, 1.0, 2.0)[:, None]
    eye = np.eye(rows_local)
    forward = np.einsum("pkw,hg->kphgw", np.stack([cos_w, -sin_w]), eye)
    forward = forward.reshape(MODES * 2 * rows_local, rows_local * grid_size)
    inverse = np.einsum("pkw,hg->gwkph", np.stack([cos_w * doubled, -sin_w * doubled]), eye)
    inverse = inverse.reshape(rows_local * grid_size, MODES * 2 * rows_local)
    column = np.stack([np.stack([cos_h, sin_h]), np.stack([-sin_h, cos_h])])
    column = column.reshape(2, 2, MODES, row_parts, rows_local)
    column = column.transpose(0, 2, 3, 1, 4).reshape(2 * MODES, row_parts * 2 * rows_local)
    as32 = lambda x: np.ascontiguousarray(x, dtype=np.float32)
    return (
        as32(forward),
        as32(forward.T),
        as32(inverse),
        as32(inverse.T),
        as32(column),
        as32(column.T),
    )


def dot_full(a, b):
    return jnp.dot(a, b, precision=HIGHEST, preferred_element_type=F32)


def halves(x):
    high = x.astype(BF16)
    return high, (x - high.astype(F32)).astype(BF16)


def dot_pairs(a, b, dims):
    spec = (dims, ((), ()))
    one = lambda x, y: lax.dot_general(x, y, spec, preferred_element_type=F32)
    return one(a[0], b[0]) + (one(a[0], b[1]) + one(a[1], b[0]))


def dot_split(table, x):
    return dot_pairs((table[0], table[1]), halves(x), NN)


def split_table(x):
    high = x.astype(jnp.bfloat16)
    low = (x - high.astype(np.float32)).astype(jnp.bfloat16)
    return np.stack([high, low])


NN = ((1,), (0,))
NT = ((1,), (1,))
TN = ((0,), (0,))


def cdf(v):
    return 0.5 + 0.5 * lax.erf(v * HALF_ROOT)


def density(v):
    return DENSITY * jnp.exp(-0.5 * v * v)


def normalise(v):
    average = jnp.mean(v, axis=-1, keepdims=True)
    centred = v - average
    spread = jnp.mean(centred * centred, axis=-1, keepdims=True)
    scale = lax.rsqrt(spread + EPS)
    return centred * scale, scale


def normal_back(unit, scale, weighted):
    m0 = jnp.mean(weighted, axis=-1, keepdims=True)
    m1 = jnp.mean(weighted * unit, axis=-1, keepdims=True)
    return scale * (weighted - m0 - unit * m1)


def call(body, grid, in_specs, out_specs, out_shape, flops, moved, name, scratch=()):
    many = isinstance(out_shape, (list, tuple))
    shapes = list(out_shape) if many else [out_shape]
    run = pl.pallas_call(
        body,
        grid=grid,
        in_specs=in_specs,
        out_specs=out_specs,
        out_shape=shapes if many else shapes[0],
        scratch_shapes=list(scratch),
        name=name,
        cost_estimate=pl.CostEstimate(
            flops=int(flops * PLANNED),
            transcendentals=0,
            bytes_accessed=int(moved * PLANNED),
        ),
        compiler_params=pltpu.CompilerParams(vmem_limit_bytes=LIMIT),
    )

    return run


def whole(shape):
    return pl.BlockSpec(shape, lambda *_: (0,) * len(shape))


def build(row_parts, item_parts):
    row_bits = row_parts.bit_length() - 1
    item_bits = item_parts.bit_length() - 1
    device_total = row_parts * item_parts
    lanes = 128

    def flip(x, bit):
        pairs = [(f, f ^ (1 << bit)) for f in range(device_total)]
        return lax.ppermute(x, AXES, pairs)

    def flip_mask(x, mask):
        pairs = [(f, f ^ mask) for f in range(device_total)]
        return lax.ppermute(x, AXES, pairs)

    core_bit = item_bits
    depth_bits = [item_bits + row_bits - 1, item_bits + row_bits - 2]
    plane_a = [item_bits + b for b in range(row_bits - 3, 0, -1)] + list(range(item_bits))
    plane_b = plane_a[::-1]
    low_bits = row_bits - 3 + item_bits
    mixing_low = list(range(low_bits))[::-1]
    masks_a, masks_b = [0], [0]
    for bit_a, bit_b in zip(plane_a, plane_b):
        masks_a = masks_a + [m | (1 << bit_a) for m in masks_a]
        masks_b = masks_b + [m | (1 << bit_b) for m in masks_b]
    place_a = [masks_a.index(m) for m in masks_b]

    def gather_stages(x, bits):
        for bit in bits:
            x = jnp.concatenate([x, flip(x, bit)], axis=0)
        return x

    def scatter_stages(x, bits, axis=0):
        for bit in bits[::-1]:
            stay, leave = jnp.split(x, 2, axis=axis)
            x = stay + flip(leave, bit)
        return x

    def mixing_order(x, index):
        for bit in range(x.shape[0].bit_length() - 1):
            lead = x.reshape((-1, 2, 1 << bit) + x.shape[1:])
            swapped = (index >> bit) % 2 == 1
            x = jnp.where(swapped, lead[:, ::-1], lead).reshape(x.shape)
        return x

    def total(x):
        for bits in ([core_bit], plane_a, depth_bits):
            masks = [0]
            for bit in bits:
                masks = masks + [m | (1 << bit) for m in masks]
            parts = [x] + [flip_mask(x, m) for m in masks[1:]]
            while len(parts) > 1:
                parts = [a + b for a, b in zip(parts[::2], parts[1::2])]
            x = parts[0]
        return x

    def local(
        frames,
        counts,
        time_weight,
        first_gain,
        first_shift,
        mixing_weight,
        mixing_bias,
        second_gain,
        second_shift,
        expand_weight,
        expand_bias,
        contract_weight,
        contract_bias,
        output_cotangent,
    ):
        items, frame_total, rows_local, width, channels = frames.shape
        grid_size = rows_local * row_parts
        tokens = rows_local * width
        wave_rows = MODES * 2 * rows_local
        groups = row_parts // PAIRS
        kept = MODES // groups
        part = kept * 2 * rows_local
        stack = 2 * rows_local
        mode_rows = kept * MODES
        shard = contract_weight.shape[0]
        hidden_total = expand_bias.shape[0]
        hidden_local = hidden_total // 2
        piece_total = len(masks_a)
        half = hidden_local // 2
        unit = half // piece_total
        quarter = half // 2
        block_size = channels // BLOCKS
        aligned = stack % 8 == 0
        tables = make_tables(grid_size, rows_local, row_parts)
        wave_fwd, wave_fwd_t, wave_inv, wave_inv_t, col, col_t = tables
        wave_fwd_t, wave_inv, wave_inv_t = map(split_table, (wave_fwd_t, wave_inv, wave_inv_t))
        col_half, col_t_half = split_table(col), split_table(col_t)

        row_index = lax.axis_index("rows")
        flat = row_index * item_parts + lax.axis_index("items")
        pair = (row_index // (row_parts // 8)) % PAIRS
        top = row_index // (row_parts // 2)
        mixing_index = top * (1 << low_bits) + flat % (1 << low_bits)
        mixing_count = 2 << low_bits

        state = []

        def seq(x):
            return after(x, *state) if state else x

        def done(x):
            state[:] = [x]

        both = jnp.concatenate([expand_weight.T, contract_weight], axis=1)
        carried = jnp.concatenate([both, mixing_weight.reshape(-1, 2 * channels)], axis=0)
        arrived = flip(carried, depth_bits[0])
        both_near = jnp.concatenate([both, flip(both, depth_bits[1])], axis=0)
        pieces = jnp.stack(
            [mixing_weight.reshape(-1, lanes), arrived[shard:].reshape(-1, lanes)]
        )
        pieces = gather_stages(pieces, mixing_low)
        axes_total = low_bits + 1

        def turn_axes(x):
            lead = x.reshape((2,) * axes_total + x.shape[1:])
            order = tuple(range(axes_total))[::-1]
            return lead.transpose(order + (axes_total, axes_total + 1)).reshape(x.shape)

        layers = mixing_order(turn_axes(pieces), mixing_index)
        layers = layers.reshape(2, 2, 2, block_size, block_size)

        def blocks_of(w):
            zero = jnp.zeros_like(w[0])
            return jnp.concatenate(
                [jnp.concatenate([w[0], zero], 1), jnp.concatenate([zero, w[1]], 1)], 0
            )

        def big(w):
            real, imag = blocks_of(w[:, 0]), blocks_of(w[:, 1])
            return jnp.concatenate(
                [jnp.concatenate([real, imag], 1), jnp.concatenate([-imag, real], 1)], 0
            )

        mix_weight = [big(layers[0]), big(layers[1])]
        bias_pairs = mixing_bias.reshape(2, 2, PAIRS, lanes)
        mix_bias = lax.dynamic_index_in_dim(bias_pairs, pair, 2, keepdims=False)
        mix_bias = mix_bias.reshape(2, 1, 2 * lanes)

        first_bit, second_bit = (1 << b for b in depth_bits)
        masks = [
            far | p | near for far in (0, first_bit) for p in masks_a for near in (0, second_bit)
        ]
        owners = flat ^ jnp.array(masks, dtype=jnp.int32)
        pick = (
            owners[:, None] == jnp.arange(device_total, dtype=jnp.int32)[None, :]
        ).astype(F32)
        bias_shards = expand_bias.reshape(device_total, shard)
        bias_local = jnp.dot(pick, bias_shards, precision=HIGHEST).reshape(1, hidden_local)

        as_row = lambda x: x.reshape(1, channels)
        gain_one, shift_one = as_row(first_gain), as_row(first_shift)
        gain_two, shift_two = as_row(second_gain), as_row(second_shift)

        def put_parts(ref, values):
            if not aligned:
                ref[0] = values
                return
            for g in range(groups):
                for p in range(PAIRS):
                    ref[g // (groups // 2), p, g % (groups // 2), 0] = values[
                        g * part : (g + 1) * part, p * lanes : (p + 1) * lanes
                    ]

        def get_parts(ref):
            if not aligned:
                return ref[0]
            rows = []
            for g in range(groups):
                rows.append(
                    jnp.concatenate(
                        [
                            ref[g // (groups // 2), p, g % (groups // 2), 0]
                            for p in range(PAIRS)
                        ],
                        axis=1,
                    )
                )
            return jnp.concatenate(rows, axis=0)

        def parts_type(count):
            shape = (2, PAIRS, groups // 2, count, part, lanes)
            if not aligned:
                shape = (count, wave_rows, channels)
            return jax.ShapeDtypeStruct(shape, F32)

        if aligned:
            parts_spec = pl.BlockSpec(
                (2, PAIRS, groups // 2, 1, part, lanes), lambda i: (0, 0, 0, i, 0, 0)
            )
        else:
            parts_spec = pl.BlockSpec((1, wave_rows, channels), lambda i: (i, 0, 0))

        def to_send(x, count):
            if aligned:
                return x
            x = x.reshape(count, 2, groups // 2, part, PAIRS, lanes)
            return x.transpose(1, 4, 2, 0, 3, 5)

        def from_send(x, count):
            x = x.reshape(2, PAIRS, groups // 2, count, part, lanes)
            if aligned:
                return x
            return x.transpose(3, 0, 2, 4, 1, 5).reshape(count, wave_rows, channels)

        def exchange(x):
            return lax.all_to_all(x.reshape(row_parts, -1, lanes), "rows", 0, 0)

        def column_type(count):
            shape = (row_parts, count, kept, stack, lanes)
            if not aligned:
                shape = (count, kept, row_parts * stack, lanes)
            return jax.ShapeDtypeStruct(shape, F32)

        if aligned:
            column_spec = pl.BlockSpec(
                (row_parts, 1, kept, stack, lanes), lambda i: (0, i, 0, 0, 0)
            )
        else:
            column_spec = pl.BlockSpec(
                (1, kept, row_parts * stack, lanes), lambda i: (i, 0, 0, 0)
            )

        def to_columns(x, count):
            x = x.reshape(row_parts, count, kept, stack, lanes)
            if aligned:
                return x
            return x.transpose(1, 2, 0, 3, 4).reshape(column_type(count).shape)

        def from_columns(x, count):
            if aligned:
                return x
            x = x.reshape(count, kept, row_parts, stack, lanes)
            return x.transpose(2, 0, 1, 3, 4)

        def get_columns(ref):
            if aligned:
                pieces = [ref[:, 0, k].reshape(row_parts * stack, lanes) for k in range(kept)]
            else:
                pieces = [ref[0, k] for k in range(kept)]
            return jnp.concatenate(pieces, axis=1)

        def put_columns(ref, values):
            for k in range(kept):
                piece = values[:, k * lanes : (k + 1) * lanes]
                if aligned:
                    ref[:, 0, k] = piece.reshape(row_parts, stack, lanes)
                else:
                    ref[0, k] = piece

        def modes_rows(m):
            cut = lambda p, k: m[p * MODES : (p + 1) * MODES, k * lanes : (k + 1) * lanes]
            return jnp.concatenate(
                [jnp.concatenate([cut(0, k), cut(1, k)], axis=1) for k in range(kept)], axis=0
            )

        def rows_modes(z):
            cut = lambda p, k: z[k * MODES : (k + 1) * MODES, p * lanes : (p + 1) * lanes]
            return jnp.concatenate(
                [jnp.concatenate([cut(0, k), cut(1, k)], axis=0) for k in range(kept)], axis=1
            )

        def live_row(counts_ref, item, f):
            seen = jnp.full((1, channels), counts_ref[item], jnp.int32)
            return jnp.where(seen > f, 1.0 / seen.astype(F32), 0.0)

        item_spec = pl.BlockSpec((1, tokens, channels), lambda i: (i, 0, 0))
        item_type = jax.ShapeDtypeStruct((items, tokens, channels), F32)
        frames_spec = pl.BlockSpec(
            (1, frame_total, rows_local, width, channels), lambda i: (i, 0, 0, 0, 0)
        )
        time_spec = whole((frame_total, channels))
        counts_spec = pl.BlockSpec(memory_space=pltpu.SMEM)
        row_spec = whole((1, channels))
        slab_bytes = tokens * channels * 4
        wave_flops = 2 * wave_rows * tokens * channels

        def head_body(counts_ref, frames_ref, time_ref, gain_ref, shift_ref, table_ref, merged_ref, parts_ref):
            item = pl.program_id(0)
            merged = 0.0
            for f in range(frame_total):
                frame = frames_ref[0, f].reshape(tokens, channels)
                merged = merged + frame * (live_row(counts_ref, item, f) * time_ref[f : f + 1, :])
            merged_ref[0] = merged
            unit, _ = normalise(merged)
            normed = unit * gain_ref[...] + shift_ref[...]
            put_parts(parts_ref, dot_full(table_ref[...], normed))

        merged, head_parts = call(
            head_body,
            (items,),
            [counts_spec, frames_spec, time_spec, row_spec, row_spec, whole(wave_fwd.shape)],
            [item_spec, parts_spec],
            [item_type, parts_type(items)],
            6 * items * wave_flops,
            items * slab_bytes * (frame_total + 2),
            "head",
        )(counts, frames, time_weight, gain_one, shift_one, wave_fwd)
        done(merged)
        columns = to_columns(exchange(to_send(head_parts, items)), items)

        far = arrived[:shard]
        batches = [seq(both_near), jnp.concatenate([far, flip(seq(far), depth_bits[1])], axis=0)]

        def gather_plane(x):
            got = {0: x}
            for bit in plane_a:
                for m in list(got):
                    got[m | (1 << bit)] = flip(got[m], bit)
            return [got[m] for m in masks_a]

        shards = [gather_plane(batches[0])]

        cot_own = output_cotangent.reshape(items * tokens, channels)
        cot_other = flip(cot_own, core_bit)
        token_total = items * tokens
        block = tokens
        token_spec = pl.BlockSpec((block, channels), lambda i: (i, 0))
        half_flops = 2 * 3 * token_total * channels * half
        count = piece_total // 2
        up_spec = pl.BlockSpec((unit, channels), lambda *_: (0, 0))
        down_spec = pl.BlockSpec((unit, channels), lambda *_: (0, 1))
        scratch_one = [pltpu.VMEM((half, channels), BF16)] * 2
        scratch_two = [pltpu.VMEM((hidden_local, channels), BF16)] * 2

        def split_into(refs, high_ref, low_ref):
            @pl.when(pl.program_id(0) == 0)
            def _():
                for n, r in enumerate(refs):
                    cut = slice(n * unit, (n + 1) * unit)
                    high_ref[cut, :], low_ref[cut, :] = halves(r[...])

        def cot_body(g1_ref, g2_ref, *refs):
            w_refs, outs, (wh, wl) = refs[:piece_total], refs[piece_total:-2], refs[-2:]
            split_into(w_refs, wh, wl)
            w = (wh[...], wl[...])
            g1, g2 = halves(g1_ref[...]), halves(g2_ref[...])
            outs[0][...] = dot_pairs(g1, w, NT)
            outs[1][...] = dot_pairs(g2, w, NT)
            if len(outs) > 2:
                outs[2][...], outs[3][...] = g1
                outs[4][...], outs[5][...] = g2

        def cot_call(w, extra):
            spec = pl.BlockSpec((block, half), lambda i: (i, 0))
            kind = jax.ShapeDtypeStruct((token_total, half), F32)
            slim_kind = jax.ShapeDtypeStruct((token_total, channels), BF16)
            out = call(
                cot_body,
                (items,),
                [token_spec, token_spec] + [down_spec] * piece_total,
                [spec, spec] + [token_spec] * extra,
                [kind, kind] + [slim_kind] * extra,
                2 * half_flops,
                token_total * (half + channels) * 8,
                "cotangent_up",
                scratch_one,
            )(cot_own, cot_other, seq(w[0]), *w[1:])
            done(out[0])
            return out

        mode_spec = pl.BlockSpec((mode_rows, 2 * lanes), lambda i: (i, 0))
        mode_type = jax.ShapeDtypeStruct((items * mode_rows, 2 * lanes), F32)
        square = (2 * lanes, 2 * lanes)
        weight_spec = whole(square)
        bias_spec = whole((2, 1, 2 * lanes))
        mix_flops = 2 * items * (2 * mode_rows * 4 * lanes * lanes + 2 * col.size * kept * lanes)

        def mix_body(x_ref, w0_ref, w1_ref, b_ref, col_ref, col_t_ref, out_ref, z_ref, u_ref, v_ref):
            z = modes_rows(dot_full(col_ref[...], get_columns(x_ref)))
            z_ref[...] = z
            u = dot_full(z, w0_ref[...]) + b_ref[0]
            u_ref[...] = u
            v = dot_full(u * cdf(u), w1_ref[...]) + b_ref[1]
            v_ref[...] = v
            mixed = v - jnp.clip(v, -SHRINK, SHRINK)
            put_columns(out_ref, dot_split(col_t_ref[...], rows_modes(mixed)))

        first_gates = [batches[1]] if 1 else []
        if 2 == 1:
            first_gates += shards[0][1:]
        if 2 == 2:
            first_gates += [s for m, s in zip(masks_a, shards[0]) if m in [1 << b for b in plane_a]]
        if 0 == 0:
            shards.append(gather_plane(batches[1]))
        mixed = call(
            mix_body,
            (items,),
            [column_spec, weight_spec, weight_spec, bias_spec]
            + [whole(col.shape), whole(col_t_half.shape)],
            [column_spec, mode_spec, mode_spec, mode_spec],
            [column_type(items), mode_type, mode_type, mode_type],
            6 * mix_flops,
            items * slab_bytes * 4,
            "mix",
        )(after(seq(columns), *first_gates), *mix_weight, mix_bias, col, col_t_half)
        done(mixed[1])
        single = [1 << b for b in plane_a]
        near = [s for m, s in zip(masks_a, shards[1]) if m in single]
        rest = [s for m, s in zip(masks_a, shards[0]) if m and m not in single]
        a1 = {0: [], 1: near + rest, 2: near, 3: near[:1], 4: near[:1] + rest}[4]
        row_back = from_send(exchange(after(from_columns(mixed[0], items), *a1)), items)

        def spatial_body(parts_ref, merged_ref, gain_ref, shift_ref, table_ref, middle_ref, normed_ref):
            middle = merged_ref[0] + dot_split(table_ref[...], get_parts(parts_ref))
            middle_ref[0] = middle
            unit, _ = normalise(middle)
            normed_ref[0] = unit * gain_ref[...] + shift_ref[...]

        def spatial_call(parts, *gates):
            out = call(
                spatial_body,
                (items,),
                [parts_spec, item_spec, row_spec, row_spec, whole(wave_inv.shape)],
                [item_spec, item_spec],
                [item_type, item_type],
                3 * items * wave_flops,
                items * slab_bytes * 4,
                "spatial",
            )(after(seq(parts), *gates), merged, gain_two, shift_two, wave_inv)
            done(out[0])
            return out

        wide = (token_total, hidden_local)
        wide_half = jax.ShapeDtypeStruct(wide, BF16)
        slim_half = jax.ShapeDtypeStruct((token_total, channels), BF16)
        wide_spec = pl.BlockSpec((tokens, hidden_local), lambda i: (i, 0))

        def feed_body(n_ref, bias_ref, ga_ref, gb_ref, *refs):
            w_refs = refs[: 2 * piece_total]
            hh, hl, ph, pl_, grad_ref, bg_ref, nh, nl, wh_ref, wl_ref = refs[2 * piece_total :]
            split_into(w_refs, wh_ref, wl_ref)

            @pl.when(pl.program_id(0) == 0)
            def _():
                bg_ref[...] = jnp.zeros_like(bg_ref)

            n = halves(n_ref[0])
            nh[...], nl[...] = n
            grad = 0.0
            for q in range(4):
                cut = slice(q * quarter, (q + 1) * quarter)
                w = (wh_ref[cut, :], wl_ref[cut, :])
                g_cut = slice(q % 2 * quarter, (q % 2 + 1) * quarter)
                raised = (ga_ref, gb_ref)[q // 2][:, g_cut]
                pre = dot_pairs(n, w, NT) + bias_ref[:, cut]
                phi = cdf(pre)
                hh[:, cut], hl[:, cut] = halves(pre * phi)
                gp = raised * (phi + pre * density(pre))
                bg_ref[:, cut] += jnp.sum(gp, axis=0, keepdims=True)
                gp = halves(gp)
                ph[:, cut], pl_[:, cut] = gp
                grad = grad + dot_pairs(gp, w, NN)
            grad_ref[0] = grad

        def feed_call(side, n):
            out = call(
                feed_body,
                (items,),
                [item_spec, whole((1, hidden_local))]
                + [pl.BlockSpec((tokens, half), lambda i: (i, 0))] * 2
                + [up_spec] * (2 * piece_total),
                [wide_spec] * 4
                + [item_spec, whole((1, hidden_local))]
                + [token_spec] * 2,
                [wide_half] * 4
                + [item_type, jax.ShapeDtypeStruct((1, hidden_local), F32)]
                + [slim_half] * 2,
                2 * 2 * 3 * token_total * channels * hidden_local,
                token_total * (hidden_local * 3 + channels * 3) * 4,
                f"feed_forward{side}",
                scratch_two,
            )(seq(n), bias_local, raised[0][side], raised[1][side], *shards[0], *shards[1])
            done(out[4])
            return out

        def middle_body(
            mid_ref, g1_ref, g2_ref, cot_ref, gain_ref, table_ref, gm_ref, parts_ref, small_ref
        ):
            unit, scale = normalise(mid_ref[0])
            grad = g1_ref[0] + g2_ref[0]
            cot = cot_ref[...]
            gm = cot + normal_back(unit, scale, grad * gain_ref[...])
            gm_ref[0] = gm
            put_parts(parts_ref, dot_split(table_ref[...], gm))

            @pl.when(pl.program_id(0) == 0)
            def _():
                small_ref[...] = jnp.zeros_like(small_ref)

            small_ref[0:1, :] += jnp.sum(grad * unit, axis=0, keepdims=True)
            small_ref[1:2, :] += jnp.sum(grad, axis=0, keepdims=True)
            small_ref[2:3, :] += jnp.sum(cot, axis=0, keepdims=True)

        small_type = jax.ShapeDtypeStruct((8, channels), F32)
        small_spec = whole((8, channels))

        if 0 == 1:
            shards.append(gather_plane(after(batches[1], mixed[1])))
        raised = [cot_call(shards[0], 4), cot_call(shards[1], 0)]
        middle, normed_own = spatial_call(row_back)
        normed_other = flip(normed_own, core_bit)
        fed = [feed_call(0, normed_own), feed_call(1, normed_other)]
        grad_middle, middle_parts, small_two = call(
            middle_body,
            (items,),
            [item_spec] * 3 + [token_spec, row_spec, whole(wave_inv_t.shape)],
            [item_spec, parts_spec, small_spec],
            [item_type, parts_type(items), small_type],
            3 * items * wave_flops,
            items * slab_bytes * 6,
            "middle_back",
        )(middle, fed[0][4], seq(flip(fed[1][4], core_bit)), cot_own, gain_two, wave_inv_t)
        done(small_two)
        grad_columns = to_columns(exchange(to_send(middle_parts, items)), items)

        lane_block = unit % lanes == 0
        wide_count = count if lane_block else 1

        def outer_body(*refs):
            out_c, out_e = refs[-2:]
            contract_out, expand_out = 0.0, 0.0
            per_side = 2 * wide_count + 6
            for s in range(2):
                mine = refs[per_side * s : per_side * (s + 1)]
                h = tuple(
                    jnp.concatenate(
                        [r[...] for r in mine[n * wide_count : (n + 1) * wide_count]], axis=1
                    )
                    for n in range(2)
                )
                ph, pl_, gh, gl, nh, nl = [r[...] for r in mine[2 * wide_count :]]
                contract_out += dot_pairs(h, (gh, gl), TN)
                expand_out += dot_pairs((ph, pl_), (nh, nl), TN)
            there = refs[2 * per_side : -2]
            if there:
                contract_out += there[0][...]
                expand_out += there[1][...]
            out_c[...], out_e[...] = contract_out, expand_out

        def outer_call(side, there=()):
            picks = place_a[side * count : (side + 1) * count]

            def unit_spec(p):
                return pl.BlockSpec((token_total, unit), lambda b: (0, b * piece_total + p))

            def gathered(x):
                return jnp.concatenate(
                    [
                        x[:, b * half + p * unit : b * half + (p + 1) * unit]
                        for b in range(2)
                        for p in picks
                    ],
                    axis=1,
                )

            def half_of(x):
                return jnp.concatenate(
                    [x[:, b * half + side * quarter :][:, :quarter] for b in range(2)], axis=1
                )

            specs, operands = [], []
            slim_spec = whole((token_total, channels))
            for s in range(2):
                values = fed[s]
                if lane_block:
                    specs += [unit_spec(p) for p in picks] * 2
                    specs += [
                        pl.BlockSpec((token_total, quarter), lambda b: (0, b * 2 + side))
                    ] * 2
                    operands += [values[0]] * count + [values[1]] * count + list(values[2:4])
                else:
                    specs += [whole((token_total, half))] * 4
                    operands += [gathered(v) for v in values[:2]]
                    operands += [half_of(v) for v in values[2:4]]
                specs += [slim_spec] * 4
                operands += list(raised[0][2 + 2 * s : 4 + 2 * s]) + list(values[6:8])
            operands[0] = seq(operands[0])
            rows = quarter if lane_block else half
            row_block = pl.BlockSpec((rows, channels), lambda b: (b, 0))
            kind = jax.ShapeDtypeStruct((half, channels), F32)
            out = call(
                outer_body,
                (half // rows,),
                specs + [row_block] * len(there),
                [row_block] * 2,
                [kind, kind],
                4 * half_flops,
                token_total * (half + channels) * 16,
                f"weight_grads{side}",
            )(*operands, *there)
            done(out[0])
            return out

        leaving = outer_call(1)
        contract_there = flip(leaving[0], plane_b[-1])
        expand_there = flip(leaving[1], plane_a[-1])

        def contract_calls():
            def down_body(hh, hl, *refs):
                extra = refs[: -3 - 2 * piece_total]
                w_refs, (out_ref, wh_ref, wl_ref) = refs[-3 - 2 * piece_total : -3], refs[-3:]
                split_into(w_refs, wh_ref, wl_ref)
                out = dot_pairs((hh[...], hl[...]), (wh_ref[...], wl_ref[...]), NN)
                if extra:
                    out = out + extra[0][0] + extra[1][0] + extra[2][...]
                out_ref[0] = out

            def down_call(side, extra, specs):
                out = call(
                    down_body,
                    (items,),
                    [wide_spec] * 2 + specs + [down_spec] * (2 * piece_total),
                    item_spec,
                    item_type,
                    2 * 3 * token_total * channels * hidden_local,
                    token_total * (hidden_local + channels) * 4,
                    f"contract{side}",
                    scratch_two,
                )(seq(fed[side][0]), fed[side][1], *extra, *shards[0], *shards[1])
                done(out)
                return out

            return down_call

        down_call = contract_calls()

        def finish_output(there):
            extra = [middle, there, as_row(contract_bias)]
            return down_call(0, extra, [item_spec, item_spec, row_spec])

        if 2:
            there = flip(down_call(1, [], []), core_bit)
        if 2 == 1:
            block_out = finish_output(there)

        def mix_back_body(
            x_ref, z_ref, u_ref, v_ref, w0_ref, w1_ref, col_ref, col_t_ref, out_ref, wg_ref, bg_ref, sum_ref
        ):
            step = pl.program_id(0)
            grad = modes_rows(dot_split(col_ref[...], get_columns(x_ref)))
            e1 = jnp.where(jnp.abs(v_ref[...]) > SHRINK, grad, 0.0)
            u = u_ref[...]
            phi = cdf(u)
            e1_half = halves(e1)
            e0 = dot_pairs(e1_half, halves(w1_ref[...]), NT) * (phi + u * density(u))
            e0_half = halves(e0)
            dz = dot_pairs(e0_half, halves(w0_ref[...]), NT)
            put_columns(out_ref, dot_split(col_t_ref[...], rows_modes(dz)))

            @pl.when(step == 0)
            def _():
                sum_ref[...] = jnp.zeros_like(sum_ref)
                bg_ref[...] = jnp.zeros_like(bg_ref)

            sum_ref[0] += dot_pairs(halves(z_ref[...]), e0_half, TN)
            sum_ref[1] += dot_pairs(halves(u * phi), e1_half, TN)
            bg_ref[0] += jnp.sum(e0, axis=0, keepdims=True)
            bg_ref[1] += jnp.sum(e1, axis=0, keepdims=True)

            @pl.when(step == items - 1)
            def _():
                for layer in range(2):
                    w = sum_ref[layer]
                    real = w[:lanes, :lanes] + w[lanes:, lanes:]
                    imag = w[:lanes, lanes:] - w[lanes:, :lanes]
                    for b in range(2):
                        cut = slice(b * block_size, (b + 1) * block_size)
                        wg_ref[layer, b, 0] = real[cut, cut]
                        wg_ref[layer, b, 1] = imag[cut, cut]

        grad_shape = (2, 2, 2, block_size, block_size)
        back_parts, mix_grad, big_bias = call(
            mix_back_body,
            (items,),
            [column_spec, mode_spec, mode_spec, mode_spec, weight_spec, weight_spec]
            + [whole(col_half.shape), whole(col_t_half.shape)],
            [column_spec, whole(grad_shape), bias_spec],
            [
                column_type(items),
                jax.ShapeDtypeStruct(grad_shape, F32),
                jax.ShapeDtypeStruct((2, 1, 2 * lanes), F32),
            ],
            3 * 2 * mix_flops,
            items * slab_bytes * 4,
            "mix_back",
            [pltpu.VMEM((2,) + square, F32)],
        )(seq(grad_columns), *mixed[1:], *mix_weight, col_half, col_t_half)
        done(big_bias)
        last_parts = from_send(exchange(from_columns(back_parts, items)), items)
        if 2 == 2:
            block_out = finish_output(there)
        staying = outer_call(0, (contract_there, expand_there))
        if 2 == 3:
            block_out = finish_output(there)
        if 2 == 0:
            block_out = finish_output(flip(down_call(1, [], []), core_bit))
        by_batch = lambda x: x.reshape(2, quarter, channels)
        contract_part = scatter_stages(by_batch(staying[0]), plane_b[:-1], 1)
        expand_part = scatter_stages(by_batch(staying[1]), plane_a[:-1], 1)

        mix_grad = mix_grad.reshape(mixing_count, -1, lanes)
        mix_grad = turn_axes(mixing_order(mix_grad, mixing_index))
        mix_grad = scatter_stages(mix_grad, mixing_low)
        joined = jnp.concatenate([expand_part, contract_part], axis=2)
        both_grad = scatter_stages(joined, depth_bits[1:], 1).reshape(2 * shard, 2 * channels)
        leaving_last = jnp.concatenate(
            [both_grad[shard:], mix_grad[1].reshape(-1, 2 * channels)], axis=0
        )
        arrived_last = flip(after(leaving_last, last_parts), depth_bits[0])
        both_grad = both_grad[:shard] + arrived_last[:shard]
        mixing_weight_grad = mix_grad[0].reshape(mixing_weight.shape) + arrived_last[
            shard:
        ].reshape(mixing_weight.shape)
        expand_weight_grad = both_grad[:, :channels].T
        contract_weight_grad = both_grad[:, channels:]

        def final_body(
            counts_ref,
            parts_ref,
            merged_ref,
            *refs,
        ):
            gm_ref, frames_ref, gain_ref, table_ref, total_ref, small_ref = refs
            item = pl.program_id(0)
            grad = dot_split(table_ref[...], get_parts(parts_ref))
            unit, scale = normalise(merged_ref[0])
            gm = gm_ref[0] + normal_back(unit, scale, grad * gain_ref[...])
            total_ref[0] = gm

            @pl.when(item == 0)
            def _():
                small_ref[...] = jnp.zeros_like(small_ref)

            small_ref[frame_total : frame_total + 1, :] += jnp.sum(
                grad * unit, axis=0, keepdims=True
            )
            small_ref[frame_total + 1 : frame_total + 2, :] += jnp.sum(
                grad, axis=0, keepdims=True
            )
            for f in range(frame_total):
                live = live_row(counts_ref, item, f)
                frame = frames_ref[0, f].reshape(tokens, channels)
                small_ref[f : f + 1, :] += live * jnp.sum(frame * gm, axis=0, keepdims=True)

        grad_merged, small_one = call(
            final_body,
            (items,),
            [counts_spec, parts_spec, item_spec, item_spec]
            + [frames_spec, row_spec, whole(wave_fwd_t.shape)],
            [item_spec, small_spec],
            [item_type, small_type],
            3 * items * wave_flops,
            items * slab_bytes * (4 + frame_total),
            "final",
        )(
            counts,
            seq(last_parts),
            merged,
            grad_middle,
            frames,
            gain_one,
            wave_fwd_t,
        )
        done(small_one)

        def frames_body(counts_ref, gm_ref, time_ref, out_ref):
            item = pl.program_id(0)
            gm = gm_ref[0]
            for f in range(frame_total):
                factor = live_row(counts_ref, item, f) * time_ref[f : f + 1, :]
                out_ref[0, f] = (gm * factor).reshape(rows_local, width, channels)

        frames_grad = call(
            frames_body,
            (items,),
            [counts_spec, item_spec, time_spec],
            frames_spec,
            jax.ShapeDtypeStruct(frames.shape, F32),
            0,
            items * slab_bytes * (1 + frame_total),
            "frames_grad",
        )(counts, seq(grad_merged), time_weight)

        bias_grad_local = fed[0][5] + fed[1][5]
        bias_full = jnp.zeros((2, 2, PAIRS, lanes), F32)
        bias_full = lax.dynamic_update_slice(
            bias_full, big_bias.reshape(2, 2, 1, lanes), (0, 0, pair, 0)
        ).reshape(4, channels)
        hidden_bias = jnp.dot(
            pick.T, bias_grad_local.reshape(-1, shard), precision=HIGHEST
        ).reshape(-1, channels)
        late = total(
            jnp.concatenate(
                [small_one[: frame_total + 2], small_two[:3], bias_full, hidden_bias], axis=0
            )
        )
        at = frame_total

        return (
            block_out.reshape(output_cotangent.shape),
            frames_grad,
            late[:at],
            late[at],
            late[at + 1],
            mixing_weight_grad,
            late[at + 5 : at + 9],
            late[at + 2],
            late[at + 3],
            expand_weight_grad,
            late[at + 9 :].reshape(hidden_total),
            contract_weight_grad,
            late[at + 4],
        )

    return local


def solution(mesh):
    return jax.shard_map(
        build(mesh.shape["rows"], mesh.shape["items"]),
        mesh=mesh,
        in_specs=(
            P("items", None, "rows", None, None),
            P("items"),
            P(),
            P(),
            P(),
            P(("rows", "items"), None),
            P(),
            P(),
            P(),
            P(None, ("rows", "items")),
            P(),
            P(("rows", "items"), None),
            P(),
            P("items", "rows", None, None),
        ),
        out_specs=(
            P("items", "rows", None, None),
            P("items", None, "rows", None, None),
            P(),
            P(),
            P(),
            P(("rows", "items"), None),
            P(),
            P(),
            P(),
            P(None, ("rows", "items")),
            P(),
            P(("rows", "items"), None),
            P(),
        ),
        check_vma=False,
    )
```

```python
import math

import jax
import jax.numpy as jnp
import numpy as np
from jax import lax
from jax.experimental import pallas as pl
from jax.experimental.pallas import tpu as pltpu
from jax.sharding import PartitionSpec as P

BLOCKS = 8
MODES = 32
PAIRS = BLOCKS // 2
HIGHEST = lax.Precision.HIGHEST
SHRINK = 0.01
EPS = 1e-05
F32 = jnp.float32
BF16 = jnp.bfloat16
AXES = ("rows", "items")
LIMIT = 56 * 1024 * 1024
HALF_ROOT = math.sqrt(0.5)
DENSITY = 1.0 / math.sqrt(2.0 * math.pi)


HELD_NOW = {}


def hold(x):
    HELD_NOW[id(x)] = x
    return x


def after(x, *others):
    out = lax.optimization_barrier((x,) + others)[0]
    return hold(out) if id(x) in HELD_NOW else out


def make_tables(grid_size, rows_local, row_parts):
    n = np.arange(grid_size)
    along = np.arange(MODES)
    across = np.concatenate(
        [np.arange(MODES // 2), np.arange(grid_size - MODES // 2, grid_size)]
    )
    step = 2.0 * np.pi / grid_size
    factor = 1.0 / np.sqrt(grid_size)
    angle = lambda k: (
        (k[:, None] * n[None, :] % grid_size).astype(np.float32) * np.float32(step)
    ).astype(np.float64)
    wide, high = angle(along), angle(across)
    cos_w, sin_w = np.cos(wide) * factor, np.sin(wide) * factor
    cos_h, sin_h = np.cos(high) * factor, np.sin(high) * factor
    doubled = np.where(along == 0, 1.0, 2.0)[:, None]
    eye = np.eye(rows_local)
    forward = np.einsum("pkw,hg->kphgw", np.stack([cos_w, -sin_w]), eye)
    forward = forward.reshape(MODES * 2 * rows_local, rows_local * grid_size)
    inverse = np.einsum("pkw,hg->gwkph", np.stack([cos_w * doubled, -sin_w * doubled]), eye)
    inverse = inverse.reshape(rows_local * grid_size, MODES * 2 * rows_local)
    column = np.stack([np.stack([cos_h, sin_h]), np.stack([-sin_h, cos_h])])
    column = column.reshape(2, 2, MODES, row_parts, rows_local)
    column = column.transpose(0, 2, 3, 1, 4).reshape(2 * MODES, row_parts * 2 * rows_local)
    as32 = lambda x: np.ascontiguousarray(x, dtype=np.float32)
    return (
        as32(forward),
        as32(forward.T),
        as32(inverse),
        as32(inverse.T),
        as32(column),
        as32(column.T),
    )


def dot_full(a, b):
    return jnp.dot(a, b, precision=HIGHEST, preferred_element_type=F32)


def halves(x):
    high = x.astype(BF16)
    return high, (x - high.astype(F32)).astype(BF16)


def dot_pairs(a, b, dims):
    spec = (dims, ((), ()))
    one = lambda x, y: lax.dot_general(x, y, spec, preferred_element_type=F32)
    return one(a[0], b[0]) + (one(a[0], b[1]) + one(a[1], b[0]))


def dot_split(table, x):
    return dot_pairs((table[0], table[1]), halves(x), NN)


def split_table(x):
    high = x.astype(jnp.bfloat16)
    low = (x - high.astype(np.float32)).astype(jnp.bfloat16)
    return np.stack([high, low])


NN = ((1,), (0,))
NT = ((1,), (1,))
TN = ((0,), (0,))


def cdf(v):
    return 0.5 + 0.5 * lax.erf(v * HALF_ROOT)


def density(v):
    return DENSITY * jnp.exp(-0.5 * v * v)


def normalise(v):
    average = jnp.mean(v, axis=-1, keepdims=True)
    centred = v - average
    spread = jnp.mean(centred * centred, axis=-1, keepdims=True)
    scale = lax.rsqrt(spread + EPS)
    return centred * scale, scale


def normal_back(unit, scale, weighted):
    m0 = jnp.mean(weighted, axis=-1, keepdims=True)
    m1 = jnp.mean(weighted * unit, axis=-1, keepdims=True)
    return scale * (weighted - m0 - unit * m1)


def call(body, grid, in_specs, out_specs, out_shape, flops, moved, name, scratch=()):
    many = isinstance(out_shape, (list, tuple))
    shapes = list(out_shape) if many else [out_shape]
    vout = VOUT.get(name, ())
    kinds = [pltpu.VMEM if n in vout else pltpu.HBM for n in range(len(shapes))]
    shapes = [k(s.shape, s.dtype) for k, s in zip(kinds, shapes)]
    run = pl.pallas_call(
        body,
        grid=grid,
        in_specs=in_specs,
        out_specs=out_specs,
        out_shape=shapes if many else shapes[0],
        scratch_shapes=list(scratch),
        name=name,
        cost_estimate=pl.CostEstimate(
            flops=int(flops),
            transcendentals=0,
            bytes_accessed=int(moved),
        ),
        compiler_params=pltpu.CompilerParams(vmem_limit_bytes=LIMIT),
    )

    def go(*operands):
        operands = [
            o
            if o.size <= 8192
            else pltpu.with_memory_space_constraint(
                o, pltpu.VMEM if id(o) in HELD_NOW else pltpu.HBM
            )
            for o in operands
        ]
        outs = run(*operands)
        for n, o in enumerate(outs if many else [outs]):
            if n in vout:
                hold(o)
        return outs

    return go


VOUT = {"spatial": (1,), "feed_forward0": (4,), "feed_forward1": (4,)}


def whole(shape):
    return pl.BlockSpec(shape, lambda *_: (0,) * len(shape))


def build(row_parts, item_parts):
    row_bits = row_parts.bit_length() - 1
    item_bits = item_parts.bit_length() - 1
    device_total = row_parts * item_parts
    lanes = 128

    def flip(x, bit):
        pairs = [(f, f ^ (1 << bit)) for f in range(device_total)]
        return lax.ppermute(x, AXES, pairs)

    def flip_mask(x, mask):
        pairs = [(f, f ^ mask) for f in range(device_total)]
        return lax.ppermute(x, AXES, pairs)

    core_bit = item_bits
    depth_bits = [item_bits + row_bits - 1, item_bits + row_bits - 2]
    plane_a = [item_bits + b for b in range(row_bits - 3, 0, -1)] + list(range(item_bits))
    plane_b = plane_a[::-1]
    low_bits = row_bits - 3 + item_bits
    mixing_low = list(range(low_bits))[::-1]
    masks_a, masks_b = [0], [0]
    for bit_a, bit_b in zip(plane_a, plane_b):
        masks_a = masks_a + [m | (1 << bit_a) for m in masks_a]
        masks_b = masks_b + [m | (1 << bit_b) for m in masks_b]
    place_a = [masks_a.index(m) for m in masks_b]

    def gather_stages(x, bits):
        for bit in bits:
            x = jnp.concatenate([x, flip(x, bit)], axis=0)
        return x

    def scatter_stages(x, bits, axis=0):
        for bit in bits[::-1]:
            stay, leave = jnp.split(x, 2, axis=axis)
            x = stay + flip(leave, bit)
        return x

    def mixing_order(x, index):
        for bit in range(x.shape[0].bit_length() - 1):
            lead = x.reshape((-1, 2, 1 << bit) + x.shape[1:])
            swapped = (index >> bit) % 2 == 1
            x = jnp.where(swapped, lead[:, ::-1], lead).reshape(x.shape)
        return x

    def total(x):
        orders = {
            0: ([core_bit], plane_a, depth_bits),
            1: (depth_bits, [core_bit], plane_a),
            2: ([core_bit], depth_bits, plane_a),
        }[1]
        for bits in orders:
            masks = [0]
            for bit in bits:
                masks = masks + [m | (1 << bit) for m in masks]
            parts = [x] + [flip_mask(x, m) for m in masks[1:]]
            if bits is orders[-1]:
                return parts
            while len(parts) > 1:
                parts = [a + b for a, b in zip(parts[::2], parts[1::2])]
            x = parts[0]

    def local(
        frames,
        counts,
        time_weight,
        first_gain,
        first_shift,
        mixing_weight,
        mixing_bias,
        second_gain,
        second_shift,
        expand_weight,
        expand_bias,
        contract_weight,
        contract_bias,
        output_cotangent,
    ):
        HELD_NOW.clear()
        items, frame_total, rows_local, width, channels = frames.shape
        grid_size = rows_local * row_parts
        tokens = rows_local * width
        wave_rows = MODES * 2 * rows_local
        groups = row_parts // PAIRS
        kept = MODES // groups
        part = kept * 2 * rows_local
        stack = 2 * rows_local
        mode_rows = kept * MODES
        shard = contract_weight.shape[0]
        hidden_total = expand_bias.shape[0]
        hidden_local = hidden_total // 2
        piece_total = len(masks_a)
        half = hidden_local // 2
        unit = half // piece_total
        quarter = half // 2
        block_size = channels // BLOCKS
        aligned = stack % 8 == 0
        tables = make_tables(grid_size, rows_local, row_parts)
        wave_fwd, wave_fwd_t, wave_inv, wave_inv_t, col, col_t = tables
        wave_fwd_t, wave_inv, wave_inv_t = map(split_table, (wave_fwd_t, wave_inv, wave_inv_t))
        col_half, col_t_half = split_table(col), split_table(col_t)

        row_index = lax.axis_index("rows")
        flat = row_index * item_parts + lax.axis_index("items")
        pair = (row_index // (row_parts // 8)) % PAIRS
        top = row_index // (row_parts // 2)
        mixing_index = top * (1 << low_bits) + flat % (1 << low_bits)
        mixing_count = 2 << low_bits

        state = []

        def seq(x):
            return after(x, *state) if state else x

        def done(x):
            state[:] = [x]

        carried = jnp.concatenate([expand_weight.T, contract_weight, mixing_weight], axis=1)
        arrived = flip(carried, depth_bits[0])
        beside = flip(carried, depth_bits[1])
        both_near = jnp.concatenate([carried[:, : 2 * channels], beside[:, : 2 * channels]], axis=0)
        pieces = jnp.stack([mixing_weight, arrived[:, 2 * channels :]])
        pieces = pieces.reshape(2, -1, lanes)
        pieces = gather_stages(pieces, mixing_low)
        axes_total = low_bits + 1

        def turn_axes(x):
            lead = x.reshape((2,) * axes_total + x.shape[1:])
            order = tuple(range(axes_total))[::-1]
            return lead.transpose(order + (axes_total, axes_total + 1)).reshape(x.shape)

        layers = mixing_order(turn_axes(pieces), mixing_index)
        layers = layers.reshape(2, 2, 2, block_size, block_size)

        def blocks_of(w):
            zero = jnp.zeros_like(w[0])
            return jnp.concatenate(
                [jnp.concatenate([w[0], zero], 1), jnp.concatenate([zero, w[1]], 1)], 0
            )

        def big(w):
            real, imag = blocks_of(w[:, 0]), blocks_of(w[:, 1])
            return jnp.concatenate(
                [jnp.concatenate([real, imag], 1), jnp.concatenate([-imag, real], 1)], 0
            )

        mix_weight = [big(layers[0]), big(layers[1])]
        bias_pairs = mixing_bias.reshape(2, 2, PAIRS, lanes)
        mix_bias = lax.dynamic_index_in_dim(bias_pairs, pair, 2, keepdims=False)
        mix_bias = mix_bias.reshape(2, 1, 2 * lanes)

        first_bit, second_bit = (1 << b for b in depth_bits)
        masks = [
            far | p | near for far in (0, first_bit) for p in masks_a for near in (0, second_bit)
        ]
        owners = flat ^ jnp.array(masks, dtype=jnp.int32)
        pick = (
            owners[:, None] == jnp.arange(device_total, dtype=jnp.int32)[None, :]
        ).astype(F32)
        bias_shards = expand_bias.reshape(device_total, shard)
        bias_local = jnp.dot(pick, bias_shards, precision=HIGHEST).reshape(1, hidden_local)

        as_row = lambda x: x.reshape(1, channels)
        gain_one, shift_one = as_row(first_gain), as_row(first_shift)
        gain_two, shift_two = as_row(second_gain), as_row(second_shift)

        def put_parts(ref, values):
            if not aligned:
                ref[0] = values
                return
            for g in range(groups):
                for p in range(PAIRS):
                    ref[g // (groups // 2), p, g % (groups // 2), 0] = values[
                        g * part : (g + 1) * part, p * lanes : (p + 1) * lanes
                    ]

        def get_parts(ref):
            if not aligned:
                return ref[0]
            rows = []
            for g in range(groups):
                rows.append(
                    jnp.concatenate(
                        [
                            ref[g // (groups // 2), p, g % (groups // 2), 0]
                            for p in range(PAIRS)
                        ],
                        axis=1,
                    )
                )
            return jnp.concatenate(rows, axis=0)

        def parts_type(count):
            shape = (2, PAIRS, groups // 2, count, part, lanes)
            if not aligned:
                shape = (count, wave_rows, channels)
            return jax.ShapeDtypeStruct(shape, F32)

        if aligned:
            parts_spec = pl.BlockSpec(
                (2, PAIRS, groups // 2, 1, part, lanes), lambda i: (0, 0, 0, i, 0, 0)
            )
        else:
            parts_spec = pl.BlockSpec((1, wave_rows, channels), lambda i: (i, 0, 0))

        def to_send(x, count):
            if aligned:
                return x
            x = x.reshape(count, 2, groups // 2, part, PAIRS, lanes)
            return x.transpose(1, 4, 2, 0, 3, 5)

        def from_send(x, count):
            x = x.reshape(2, PAIRS, groups // 2, count, part, lanes)
            if aligned:
                return x
            return x.transpose(3, 0, 2, 4, 1, 5).reshape(count, wave_rows, channels)

        def exchange(x):
            return lax.all_to_all(x.reshape(row_parts, -1, lanes), "rows", 0, 0)

        def column_type(count):
            shape = (row_parts, count, kept, stack, lanes)
            if not aligned:
                shape = (count, kept, row_parts * stack, lanes)
            return jax.ShapeDtypeStruct(shape, F32)

        if aligned:
            column_spec = pl.BlockSpec(
                (row_parts, 1, kept, stack, lanes), lambda i: (0, i, 0, 0, 0)
            )
        else:
            column_spec = pl.BlockSpec(
                (1, kept, row_parts * stack, lanes), lambda i: (i, 0, 0, 0)
            )

        def to_columns(x, count):
            x = x.reshape(row_parts, count, kept, stack, lanes)
            if aligned:
                return x
            return x.transpose(1, 2, 0, 3, 4).reshape(column_type(count).shape)

        def from_columns(x, count):
            if aligned:
                return x
            x = x.reshape(count, kept, row_parts, stack, lanes)
            return x.transpose(2, 0, 1, 3, 4)

        def get_columns(ref):
            if aligned:
                pieces = [ref[:, 0, k].reshape(row_parts * stack, lanes) for k in range(kept)]
            else:
                pieces = [ref[0, k] for k in range(kept)]
            return jnp.concatenate(pieces, axis=1)

        def put_columns(ref, values):
            for k in range(kept):
                piece = values[:, k * lanes : (k + 1) * lanes]
                if aligned:
                    ref[:, 0, k] = piece.reshape(row_parts, stack, lanes)
                else:
                    ref[0, k] = piece

        def modes_rows(m):
            cut = lambda p, k: m[p * MODES : (p + 1) * MODES, k * lanes : (k + 1) * lanes]
            return jnp.concatenate(
                [jnp.concatenate([cut(0, k), cut(1, k)], axis=1) for k in range(kept)], axis=0
            )

        def rows_modes(z):
            cut = lambda p, k: z[k * MODES : (k + 1) * MODES, p * lanes : (p + 1) * lanes]
            return jnp.concatenate(
                [jnp.concatenate([cut(0, k), cut(1, k)], axis=0) for k in range(kept)], axis=1
            )

        def live_row(counts_ref, item, f):
            seen = jnp.full((1, channels), counts_ref[item], jnp.int32)
            return jnp.where(seen > f, 1.0 / seen.astype(F32), 0.0)

        item_spec = pl.BlockSpec((1, tokens, channels), lambda i: (i, 0, 0))
        item_type = jax.ShapeDtypeStruct((items, tokens, channels), F32)
        frames_spec = pl.BlockSpec(
            (1, frame_total, rows_local, width, channels), lambda i: (i, 0, 0, 0, 0)
        )
        time_spec = whole((frame_total, channels))
        counts_spec = pl.BlockSpec(memory_space=pltpu.SMEM)
        row_spec = whole((1, channels))
        slab_bytes = tokens * channels * 4
        wave_flops = 2 * wave_rows * tokens * channels

        def head_body(counts_ref, frames_ref, time_ref, gain_ref, shift_ref, table_ref, merged_ref, parts_ref):
            item = pl.program_id(0)
            merged = 0.0
            for f in range(frame_total):
                frame = frames_ref[0, f].reshape(tokens, channels)
                merged = merged + frame * (live_row(counts_ref, item, f) * time_ref[f : f + 1, :])
            merged_ref[0] = merged
            unit, _ = normalise(merged)
            normed = unit * gain_ref[...] + shift_ref[...]
            put_parts(parts_ref, dot_full(table_ref[...], normed))

        merged, head_parts = call(
            head_body,
            (items,),
            [counts_spec, frames_spec, time_spec, row_spec, row_spec, whole(wave_fwd.shape)],
            [item_spec, parts_spec],
            [item_type, parts_type(items)],
            6 * items * wave_flops,
            items * slab_bytes * (frame_total + 2),
            "head",
        )(counts, frames, time_weight, gain_one, shift_one, wave_fwd)
        done(merged)
        columns = hold(to_columns(exchange(to_send(head_parts, items)), items))

        far = arrived[:, : 2 * channels]
        batches = [seq(both_near), jnp.concatenate([far, flip(seq(far), depth_bits[1])], axis=0)]

        def gather_plane(x):
            got = {0: x}
            for bit in plane_a:
                for m in list(got):
                    got[m | (1 << bit)] = flip(got[m], bit)
            return [got[m] for m in masks_a]

        shards = [gather_plane(batches[0])]

        cot_own = output_cotangent.reshape(items * tokens, channels)
        cot_other = hold(flip(cot_own, core_bit))
        token_total = items * tokens
        block = tokens
        token_spec = pl.BlockSpec((block, channels), lambda i: (i, 0))
        half_flops = 2 * 3 * token_total * channels * half
        count = piece_total // 2
        up_spec = pl.BlockSpec((unit, channels), lambda *_: (0, 0))
        down_spec = pl.BlockSpec((unit, channels), lambda *_: (0, 1))
        scratch_one = [pltpu.VMEM((half, channels), BF16)] * 2
        scratch_two = [pltpu.VMEM((hidden_local, channels), BF16)] * 2

        def split_into(refs, high_ref, low_ref):
            @pl.when(pl.program_id(0) == 0)
            def _():
                for n, r in enumerate(refs):
                    cut = slice(n * unit, (n + 1) * unit)
                    high_ref[cut, :], low_ref[cut, :] = halves(r[...])

        def cot_body(g1_ref, g2_ref, *refs):
            w_refs, outs, (wh, wl) = refs[:piece_total], refs[piece_total:-2], refs[-2:]
            split_into(w_refs, wh, wl)
            w = (wh[...], wl[...])
            g1, g2 = halves(g1_ref[...]), halves(g2_ref[...])
            outs[0][...] = dot_pairs(g1, w, NT)
            outs[1][...] = dot_pairs(g2, w, NT)
            if len(outs) > 2:
                outs[2][...], outs[3][...] = g1
                outs[4][...], outs[5][...] = g2

        def cot_call(w, extra):
            spec = pl.BlockSpec((block, half), lambda i: (i, 0))
            kind = jax.ShapeDtypeStruct((token_total, half), F32)
            slim_kind = jax.ShapeDtypeStruct((token_total, channels), BF16)
            out = call(
                cot_body,
                (items,),
                [token_spec, token_spec] + [down_spec] * piece_total,
                [spec, spec] + [token_spec] * extra,
                [kind, kind] + [slim_kind] * extra,
                2 * half_flops,
                token_total * (half + channels) * 8,
                "cotangent_up",
                scratch_one,
            )(cot_own, cot_other, seq(w[0]), *w[1:])
            done(out[0])
            return out

        mode_spec = pl.BlockSpec((mode_rows, 2 * lanes), lambda i: (i, 0))
        mode_type = jax.ShapeDtypeStruct((items * mode_rows, 2 * lanes), F32)
        square = (2 * lanes, 2 * lanes)
        weight_spec = whole(square)
        bias_spec = whole((2, 1, 2 * lanes))
        mix_flops = 2 * items * (2 * mode_rows * 4 * lanes * lanes + 2 * col.size * kept * lanes)

        def layer(z, w):
            zr, zi = z[:, :lanes], z[:, lanes:]
            real = dot_full(zr, w[:lanes, :lanes]) + dot_full(zi, w[lanes:, :lanes])
            imag = dot_full(zi, w[lanes:, lanes:]) + dot_full(zr, w[:lanes, lanes:])
            return jnp.concatenate([real, imag], axis=1)

        same = (np.arange(2 * MODES) // MODES)[:, None] == (
            np.arange(col.shape[1]) // rows_local % 2
        )[None, :]
        col_two = np.stack([np.where(same, col, 0), np.where(same, 0, col)]).astype(np.float32)

        def mix_body(x_ref, w0_ref, w1_ref, b_ref, col_ref, col_t_ref, out_ref, z_ref, u_ref, v_ref):
            x = get_columns(x_ref)
            z = modes_rows(dot_full(col_ref[0], x) + dot_full(col_ref[1], x))
            z_ref[...] = z
            u = layer(z, w0_ref[...]) + b_ref[0]
            u_ref[...] = u
            v = layer(u * cdf(u), w1_ref[...]) + b_ref[1]
            v_ref[...] = v
            mixed = v - jnp.clip(v, -SHRINK, SHRINK)
            put_columns(out_ref, dot_split(col_t_ref[...], rows_modes(mixed)))

        first_gates = [batches[1]] if 1 else []
        if 2 == 1:
            first_gates += shards[0][1:]
        if 2 == 2:
            first_gates += [s for m, s in zip(masks_a, shards[0]) if m in [1 << b for b in plane_a]]
        if 0 == 0:
            shards.append(gather_plane(batches[1]))
        mixed = call(
            mix_body,
            (items,),
            [column_spec, weight_spec, weight_spec, bias_spec]
            + [whole(col_two.shape), whole(col_t_half.shape)],
            [column_spec, mode_spec, mode_spec, mode_spec],
            [column_type(items), mode_type, mode_type, mode_type],
            6 * mix_flops,
            items * slab_bytes * 4,
            "mix",
        )(after(seq(columns), *first_gates), *mix_weight, mix_bias, col_two, col_t_half)
        done(mixed[1])
        single = [1 << b for b in plane_a]
        near = [s for m, s in zip(masks_a, shards[1]) if m in single]
        rest = [s for m, s in zip(masks_a, shards[0]) if m and m not in single]
        a1 = {0: [], 1: near + rest, 2: near, 3: near[:1], 4: near[:1] + rest}[4]
        row_back = hold(from_send(exchange(after(from_columns(mixed[0], items), *a1)), items))

        def spatial_body(parts_ref, merged_ref, gain_ref, shift_ref, table_ref, middle_ref, normed_ref):
            middle = merged_ref[0] + dot_split(table_ref[...], get_parts(parts_ref))
            middle_ref[0] = middle
            unit, _ = normalise(middle)
            normed_ref[0] = unit * gain_ref[...] + shift_ref[...]

        def spatial_call(parts, *gates):
            out = call(
                spatial_body,
                (items,),
                [parts_spec, item_spec, row_spec, row_spec, whole(wave_inv.shape)],
                [item_spec, item_spec],
                [item_type, item_type],
                3 * items * wave_flops,
                items * slab_bytes * 4,
                "spatial",
            )(after(seq(parts), *gates), merged, gain_two, shift_two, wave_inv)
            done(out[0])
            return out

        wide = (token_total, hidden_local)
        wide_half = jax.ShapeDtypeStruct(wide, BF16)
        slim_half = jax.ShapeDtypeStruct((token_total, channels), BF16)
        wide_spec = pl.BlockSpec((tokens, hidden_local), lambda i: (i, 0))

        def feed_body(n_ref, bias_ref, ga_ref, gb_ref, *refs):
            w_refs = refs[: 2 * piece_total]
            hh, hl, ph, pl_, grad_ref, bg_ref, nh, nl, wh_ref, wl_ref = refs[2 * piece_total :]
            split_into(w_refs, wh_ref, wl_ref)

            @pl.when(pl.program_id(0) == 0)
            def _():
                bg_ref[...] = jnp.zeros_like(bg_ref)

            n = halves(n_ref[0])
            nh[...], nl[...] = n
            grad = 0.0
            for q in range(4):
                cut = slice(q * quarter, (q + 1) * quarter)
                w = (wh_ref[cut, :], wl_ref[cut, :])
                g_cut = slice(q % 2 * quarter, (q % 2 + 1) * quarter)
                raised = (ga_ref, gb_ref)[q // 2][:, g_cut]
                pre = dot_pairs(n, w, NT) + bias_ref[:, cut]
                phi = cdf(pre)
                hh[:, cut], hl[:, cut] = halves(pre * phi)
                gp = raised * (phi + pre * density(pre))
                bg_ref[:, cut] += jnp.sum(gp, axis=0, keepdims=True)
                gp = halves(gp)
                ph[:, cut], pl_[:, cut] = gp
                grad = grad + dot_pairs(gp, w, NN)
            grad_ref[0] = grad

        def feed_call(side, n):
            out = call(
                feed_body,
                (items,),
                [item_spec, whole((1, hidden_local))]
                + [pl.BlockSpec((tokens, half), lambda i: (i, 0))] * 2
                + [up_spec] * (2 * piece_total),
                [wide_spec] * 4
                + [item_spec, whole((1, hidden_local))]
                + [token_spec] * 2,
                [wide_half] * 4
                + [item_type, jax.ShapeDtypeStruct((1, hidden_local), F32)]
                + [slim_half] * 2,
                2 * 2 * 3 * token_total * channels * hidden_local,
                token_total * (hidden_local * 3 + channels * 3) * 4,
                f"feed_forward{side}",
                scratch_two,
            )(seq(n), bias_local, raised[0][side], raised[1][side], *shards[0], *shards[1])
            done(out[4])
            return out

        def middle_body(
            mid_ref, g1_ref, g2_ref, cot_ref, gain_ref, table_ref, gm_ref, parts_ref, small_ref
        ):
            unit, scale = normalise(mid_ref[0])
            grad = g1_ref[0] + g2_ref[0]
            cot = cot_ref[...]
            gm = cot + normal_back(unit, scale, grad * gain_ref[...])
            gm_ref[0] = gm
            put_parts(parts_ref, dot_split(table_ref[...], gm))

            @pl.when(pl.program_id(0) == 0)
            def _():
                small_ref[...] = jnp.zeros_like(small_ref)

            small_ref[0:1, :] += jnp.sum(grad * unit, axis=0, keepdims=True)
            small_ref[1:2, :] += jnp.sum(grad, axis=0, keepdims=True)
            small_ref[2:3, :] += jnp.sum(cot, axis=0, keepdims=True)

        small_type = jax.ShapeDtypeStruct((8, channels), F32)
        small_spec = whole((8, channels))

        if 0 == 1:
            shards.append(gather_plane(after(batches[1], mixed[1])))
        raised = [cot_call(shards[0], 4)]
        if not 0:
            raised.append(cot_call(shards[1], 0))
        middle, normed_own = spatial_call(row_back)
        normed_other = hold(flip(normed_own, core_bit))
        if 0:
            raised.append(cot_call(shards[1], 0))
        fed = [feed_call(0, normed_own), feed_call(1, normed_other)]
        grad_middle, middle_parts, small_two = call(
            middle_body,
            (items,),
            [item_spec] * 3 + [token_spec, row_spec, whole(wave_inv_t.shape)],
            [item_spec, parts_spec, small_spec],
            [item_type, parts_type(items), small_type],
            3 * items * wave_flops,
            items * slab_bytes * 6,
            "middle_back",
        )(middle, fed[0][4], seq(hold(flip(fed[1][4], core_bit))), cot_own, gain_two, wave_inv_t)
        done(small_two)
        grad_columns = hold(to_columns(exchange(to_send(middle_parts, items)), items))

        lane_block = unit % lanes == 0
        wide_count = count if lane_block else 1

        def outer_body(*refs):
            outs = refs[-4:] if refs[-1].ndim == 3 else refs[-2:]
            contract_out, expand_out = 0.0, 0.0
            per_side = 2 * wide_count + 6
            for s in range(2):
                mine = refs[per_side * s : per_side * (s + 1)]
                h = tuple(
                    jnp.concatenate(
                        [r[...] for r in mine[n * wide_count : (n + 1) * wide_count]], axis=1
                    )
                    for n in range(2)
                )
                ph, pl_, gh, gl, nh, nl = [r[...] for r in mine[2 * wide_count :]]
                contract_out += dot_pairs(h, (gh, gl), TN)
                expand_out += dot_pairs((ph, pl_), (nh, nl), TN)
            if len(outs) == 4:
                for o, x in ((0, contract_out), (2, expand_out)):
                    for side in range(2):
                        for b in range(outs[0].shape[0]):
                            at = (b * 2 + side) * outs[0].shape[1]
                            outs[o + side][b] = x[at : at + outs[0].shape[1], :]
            else:
                outs[0][...], outs[1][...] = contract_out, expand_out

        def outer_call(side):
            picks = place_a[side * count : (side + 1) * count]

            def unit_spec(p):
                return pl.BlockSpec((token_total, unit), lambda b: (0, b * piece_total + p))

            def gathered(x):
                return jnp.concatenate(
                    [
                        x[:, b * half + p * unit : b * half + (p + 1) * unit]
                        for b in range(2)
                        for p in picks
                    ],
                    axis=1,
                )

            def half_of(x):
                return jnp.concatenate(
                    [x[:, b * half + side * quarter :][:, :quarter] for b in range(2)], axis=1
                )

            specs, operands = [], []
            slim_spec = whole((token_total, channels))
            for s in range(2):
                values = fed[s]
                if lane_block:
                    specs += [unit_spec(p) for p in picks] * 2
                    specs += [
                        pl.BlockSpec((token_total, quarter), lambda b: (0, b * 2 + side))
                    ] * 2
                    operands += [values[0]] * count + [values[1]] * count + list(values[2:4])
                else:
                    specs += [whole((token_total, half))] * 4
                    operands += [gathered(v) for v in values[:2]]
                    operands += [half_of(v) for v in values[2:4]]
                specs += [slim_spec] * 4
                operands += list(raised[0][2 + 2 * s : 4 + 2 * s]) + list(values[6:8])
            operands[0] = seq(operands[0])
            rows = quarter if lane_block else half
            row_block = pl.BlockSpec((rows, channels), lambda b: (b, 0))
            if side == 0:
                eighth = quarter // 2
                outs = [jax.ShapeDtypeStruct((2, eighth, channels), F32)] * 4
                batches_here = rows // quarter
                out_specs = [
                    pl.BlockSpec((batches_here, eighth, channels), lambda b: (b, 0, 0))
                ] * 4
            else:
                outs = [jax.ShapeDtypeStruct((half, channels), F32)] * 2
                out_specs = [row_block] * 2
            out = call(
                outer_body,
                (half // rows,),
                specs,
                out_specs,
                outs,
                4 * half_flops,
                token_total * (half + channels) * 16,
                f"weight_grads{side}",
            )(*operands)
            done(out[0])
            return out

        leaving = outer_call(1)
        staying = outer_call(0) if 1 else None
        contract_there = hold(flip(leaving[0], plane_b[-1]))
        expand_there = hold(flip(leaving[1], plane_a[-1]))

        def contract_calls():
            def down_body(hh, hl, *refs):
                extra = refs[: -3 - 2 * piece_total]
                w_refs, (out_ref, wh_ref, wl_ref) = refs[-3 - 2 * piece_total : -3], refs[-3:]
                split_into(w_refs, wh_ref, wl_ref)
                out = dot_pairs((hh[...], hl[...]), (wh_ref[...], wl_ref[...]), NN)
                if extra:
                    out = out + extra[0][0] + extra[1][0] + extra[2][...]
                out_ref[0] = out

            def down_call(side, extra, specs):
                out = call(
                    down_body,
                    (items,),
                    [wide_spec] * 2 + specs + [down_spec] * (2 * piece_total),
                    item_spec,
                    item_type,
                    2 * 3 * token_total * channels * hidden_local,
                    token_total * (hidden_local + channels) * 4,
                    f"contract{side}",
                    scratch_two,
                )(seq(fed[side][0]), fed[side][1], *extra, *shards[0], *shards[1])
                done(out)
                return out

            return down_call

        down_call = contract_calls()

        def finish_output(there):
            extra = [middle, there, as_row(contract_bias)]
            return down_call(0, extra, [item_spec, item_spec, row_spec])

        if 4 in (1, 2, 3):
            there = hold(flip(down_call(1, [], []), core_bit))
        if 4 == 1:
            block_out = finish_output(there)

        def mix_back_body(
            x_ref, z_ref, u_ref, v_ref, w0_ref, w1_ref, col_ref, col_t_ref, out_ref, wg_ref, bg_ref, sum_ref
        ):
            step = pl.program_id(0)
            grad = modes_rows(dot_split(col_ref[...], get_columns(x_ref)))
            e1 = jnp.where(jnp.abs(v_ref[...]) > SHRINK, grad, 0.0)
            u = u_ref[...]
            phi = cdf(u)
            e1_half = halves(e1)
            e0 = dot_pairs(e1_half, halves(w1_ref[...]), NT) * (phi + u * density(u))
            e0_half = halves(e0)
            dz = dot_pairs(e0_half, halves(w0_ref[...]), NT)
            put_columns(out_ref, dot_split(col_t_ref[...], rows_modes(dz)))

            @pl.when(step == 0)
            def _():
                sum_ref[...] = jnp.zeros_like(sum_ref)
                bg_ref[...] = jnp.zeros_like(bg_ref)

            sum_ref[0] += dot_pairs(halves(z_ref[...]), e0_half, TN)
            sum_ref[1] += dot_pairs(halves(u * phi), e1_half, TN)
            bg_ref[0] += jnp.sum(e0, axis=0, keepdims=True)
            bg_ref[1] += jnp.sum(e1, axis=0, keepdims=True)

            @pl.when(step == items - 1)
            def _():
                for layer in range(2):
                    w = sum_ref[layer]
                    real = w[:lanes, :lanes] + w[lanes:, lanes:]
                    imag = w[:lanes, lanes:] - w[lanes:, :lanes]
                    for b in range(2):
                        cut = slice(b * block_size, (b + 1) * block_size)
                        wg_ref[layer, b, 0] = real[cut, cut]
                        wg_ref[layer, b, 1] = imag[cut, cut]

        grad_shape = (2, 2, 2, block_size, block_size)
        back_parts, mix_grad, big_bias = call(
            mix_back_body,
            (items,),
            [column_spec, mode_spec, mode_spec, mode_spec, weight_spec, weight_spec]
            + [whole(col_half.shape), whole(col_t_half.shape)],
            [column_spec, whole(grad_shape), bias_spec],
            [
                column_type(items),
                jax.ShapeDtypeStruct(grad_shape, F32),
                jax.ShapeDtypeStruct((2, 1, 2 * lanes), F32),
            ],
            3 * 2 * mix_flops,
            items * slab_bytes * 4,
            "mix_back",
            [pltpu.VMEM((2,) + square, F32)],
        )(seq(grad_columns), *mixed[1:], *mix_weight, col_half, col_t_half)
        done(big_bias)
        last_parts = hold(from_send(exchange(from_columns(back_parts, items)), items))
        if 4 == 2:
            block_out = finish_output(there)
        if staying is None:
            staying = outer_call(0)
        came = [x.reshape(2, quarter, channels) for x in (contract_there, expand_there)]
        if 4 == 4:
            there = hold(flip(down_call(1, [], []), core_bit))

        def add_body(a_ref, b_ref, c_ref, d_ref, o1_ref, o2_ref):
            o1_ref[...] = a_ref[...] + b_ref[...]
            o2_ref[...] = c_ref[...] + d_ref[...]

        thin = (1, quarter // 2, channels)
        first_part = pl.BlockSpec(thin, lambda b: (b, 0, 0))
        second_part = pl.BlockSpec(thin, lambda b: (b, 1, 0))
        leave_kind = jax.ShapeDtypeStruct((2, quarter // 2, channels), F32)
        leave_c, leave_e = call(
            add_body,
            (2,),
            [first_part, second_part] * 2,
            [first_part] * 2,
            [leave_kind] * 2,
            0,
            half * channels * 12,
            "add_leaving",
        )(seq(staying[1]), came[0], staying[3], came[1])
        done(leave_c)
        if 4 == 3:
            block_out = finish_output(there)
        if 4 == 4 and 1:
            block_out = finish_output(there)
        travelling = []
        for stay, leave, got, bits in (
            (staying[2], leave_e, came[1], plane_a),
            (staying[0], leave_c, came[0], plane_b),
        ):
            stay = stay + got[:, : quarter // 2]
            for bit in bits[1:-1][::-1]:
                stay, leave = jnp.split(stay + flip(leave, bit), 2, axis=1)
            travelling.append((stay, flip(leave, bits[0])))
        if 4 == 0:
            block_out = finish_output(hold(flip(down_call(1, [], []), core_bit)))

        mix_grad = mix_grad.reshape(mixing_count, -1, lanes)
        mix_grad = turn_axes(mixing_order(mix_grad, mixing_index))
        if 1:
            mix_grad = after(mix_grad, block_out)
        mix_grad = scatter_stages(mix_grad, mixing_low)
        def final_body(
            counts_ref,
            parts_ref,
            merged_ref,
            *refs,
        ):
            gm_ref, frames_ref, gain_ref, table_ref, total_ref, small_ref = refs
            item = pl.program_id(0)
            grad = dot_split(table_ref[...], get_parts(parts_ref))
            unit, scale = normalise(merged_ref[0])
            gm = gm_ref[0] + normal_back(unit, scale, grad * gain_ref[...])
            total_ref[0] = gm

            @pl.when(item == 0)
            def _():
                small_ref[...] = jnp.zeros_like(small_ref)

            small_ref[frame_total : frame_total + 1, :] += jnp.sum(
                grad * unit, axis=0, keepdims=True
            )
            small_ref[frame_total + 1 : frame_total + 2, :] += jnp.sum(
                grad, axis=0, keepdims=True
            )
            for f in range(frame_total):
                live = live_row(counts_ref, item, f)
                frame = frames_ref[0, f].reshape(tokens, channels)
                small_ref[f : f + 1, :] += live * jnp.sum(frame * gm, axis=0, keepdims=True)

        grad_merged, small_one = call(
            final_body,
            (items,),
            [counts_spec, parts_spec, item_spec, item_spec]
            + [frames_spec, row_spec, whole(wave_fwd_t.shape)],
            [item_spec, small_spec],
            [item_type, small_type],
            3 * items * wave_flops,
            items * slab_bytes * (4 + frame_total),
            "final",
        )(
            counts,
            seq(last_parts),
            merged,
            grad_middle,
            frames,
            gain_one,
            wave_fwd_t,
        )
        done(small_one)

        def frames_body(counts_ref, gm_ref, time_ref, out_ref):
            item = pl.program_id(0)
            gm = gm_ref[0]
            for f in range(frame_total):
                factor = live_row(counts_ref, item, f) * time_ref[f : f + 1, :]
                out_ref[0, f] = (gm * factor).reshape(rows_local, width, channels)

        frames_grad = call(
            frames_body,
            (items,),
            [counts_spec, item_spec, time_spec],
            frames_spec,
            jax.ShapeDtypeStruct(frames.shape, F32),
            0,
            items * slab_bytes * (1 + frame_total),
            "frames_grad",
        )(counts, seq(grad_merged), time_weight)

        if 1:
            gate = small_one if 1 == 1 else block_out
            travelling = [(s, after(r, gate)) for s, r in travelling]
        joined = jnp.concatenate([s + r for s, r in travelling], axis=2)
        stay, leave = jnp.split(joined, 2, axis=1)
        got = flip(leave, depth_bits[1])
        if 1:
            got = after(got, small_one)
        both_grad = (stay + got).reshape(2 * shard, 2 * channels)
        leaving_last = jnp.concatenate(
            [both_grad[shard:], mix_grad[1].reshape(-1, 2 * channels)], axis=0
        )
        arrived_last = flip(after(leaving_last, last_parts), depth_bits[0])
        both_grad = both_grad[:shard] + arrived_last[:shard]
        mixing_weight_grad = mix_grad[0].reshape(mixing_weight.shape) + arrived_last[
            shard:
        ].reshape(mixing_weight.shape)
        expand_weight_grad = both_grad[:, :channels].T
        contract_weight_grad = both_grad[:, channels:]

        bias_grad_local = fed[0][5] + fed[1][5]
        bias_full = jnp.zeros((2, 2, PAIRS, lanes), F32)
        bias_full = lax.dynamic_update_slice(
            bias_full, big_bias.reshape(2, 2, 1, lanes), (0, 0, pair, 0)
        ).reshape(4, channels)
        hidden_bias = jnp.dot(
            pick.T, bias_grad_local.reshape(-1, shard), precision=HIGHEST
        ).reshape(-1, channels)
        at = frame_total
        rows = jnp.concatenate(
            [small_one[: at + 2], small_two[:3], bias_full, hidden_bias], axis=0
        )
        parts = total(rows)
        widths = [at, 1, 1, 1, 1, 1, 4, rows.shape[0] - at - 9]

        def finish_body(*refs):
            ins, outs = refs[: len(parts)], refs[len(parts) :]
            sums = [r[...] for r in ins]
            while len(sums) > 1:
                sums = [a + b for a, b in zip(sums[::2], sums[1::2])]
            row = 0
            for out, count in zip(outs, widths):
                out[...] = sums[0][row : row + count, :]
                row += count

        finals = call(
            finish_body,
            (1,),
            [whole(rows.shape)] * len(parts),
            [whole((w, channels)) for w in widths],
            [jax.ShapeDtypeStruct((w, channels), F32) for w in widths],
            0,
            rows.size * 24,
            "sums",
        )(*parts)
        time_grad, gain_1, shift_1, gain_2, shift_2, bias_c, mix_bias_grad, bias_e = finals

        return (
            block_out.reshape(output_cotangent.shape),
            frames_grad,
            time_grad,
            gain_1.reshape(channels),
            shift_1.reshape(channels),
            mixing_weight_grad,
            mix_bias_grad,
            gain_2.reshape(channels),
            shift_2.reshape(channels),
            expand_weight_grad,
            bias_e.reshape(hidden_total),
            contract_weight_grad,
            bias_c.reshape(channels),
        )

    return local


def solution(mesh):
    return jax.shard_map(
        build(mesh.shape["rows"], mesh.shape["items"]),
        mesh=mesh,
        in_specs=(
            P("items", None, "rows", None, None),
            P("items"),
            P(),
            P(),
            P(),
            P(("rows", "items"), None),
            P(),
            P(),
            P(),
            P(None, ("rows", "items")),
            P(),
            P(("rows", "items"), None),
            P(),
            P("items", "rows", None, None),
        ),
        out_specs=(
            P("items", "rows", None, None),
            P("items", None, "rows", None, None),
            P(),
            P(),
            P(),
            P(("rows", "items"), None),
            P(),
            P(),
            P(),
            P(None, ("rows", "items")),
            P(),
            P(("rows", "items"), None),
            P(),
        ),
        check_vma=False,
    )
```

```python
import math

import jax
import jax.numpy as jnp
import numpy as np
from jax import lax
from jax.experimental import pallas as pl
from jax.experimental.pallas import tpu as pltpu
from jax.sharding import PartitionSpec as P

BLOCKS = 8
MODES = 32
PAIRS = BLOCKS // 2
HIGHEST = lax.Precision.HIGHEST
SHRINK = 0.01
EPS = 1e-05
F32 = jnp.float32
BF16 = jnp.bfloat16
AXES = ("rows", "items")
LIMIT = 56 * 1024 * 1024
HALF_ROOT = math.sqrt(0.5)
DENSITY = 1.0 / math.sqrt(2.0 * math.pi)


HELD_NOW = {}


def hold(x):
    HELD_NOW[id(x)] = x
    return x


def after(x, *others):
    out = lax.optimization_barrier((x,) + others)[0]
    return hold(out) if id(x) in HELD_NOW else out


def make_tables(grid_size, rows_local, row_parts):
    n = np.arange(grid_size)
    along = np.arange(MODES)
    across = np.concatenate(
        [np.arange(MODES // 2), np.arange(grid_size - MODES // 2, grid_size)]
    )
    step = 2.0 * np.pi / grid_size
    factor = 1.0 / np.sqrt(grid_size)
    angle = lambda k: (
        (k[:, None] * n[None, :] % grid_size).astype(np.float32) * np.float32(step)
    ).astype(np.float64)
    wide, high = angle(along), angle(across)
    cos_w, sin_w = np.cos(wide) * factor, np.sin(wide) * factor
    cos_h, sin_h = np.cos(high) * factor, np.sin(high) * factor
    doubled = np.where(along == 0, 1.0, 2.0)[:, None]
    eye = np.eye(rows_local)
    forward = np.einsum("pkw,hg->kphgw", np.stack([cos_w, -sin_w]), eye)
    forward = forward.reshape(MODES * 2 * rows_local, rows_local * grid_size)
    inverse = np.einsum("pkw,hg->gwkph", np.stack([cos_w * doubled, -sin_w * doubled]), eye)
    inverse = inverse.reshape(rows_local * grid_size, MODES * 2 * rows_local)
    column = np.stack([np.stack([cos_h, sin_h]), np.stack([-sin_h, cos_h])])
    column = column.reshape(2, 2, MODES, row_parts, rows_local)
    column = column.transpose(0, 2, 3, 1, 4).reshape(2 * MODES, row_parts * 2 * rows_local)
    as32 = lambda x: np.ascontiguousarray(x, dtype=np.float32)
    return (
        as32(forward),
        as32(forward.T),
        as32(inverse),
        as32(inverse.T),
        as32(column),
        as32(column.T),
    )


def dot_full(a, b):
    return jnp.dot(a, b, precision=HIGHEST, preferred_element_type=F32)


def halves(x):
    high = x.astype(BF16)
    return high, (x - high.astype(F32)).astype(BF16)


def dot_pairs(a, b, dims):
    spec = (dims, ((), ()))
    one = lambda x, y: lax.dot_general(x, y, spec, preferred_element_type=F32)
    return one(a[0], b[0]) + (one(a[0], b[1]) + one(a[1], b[0]))


def dot_split(table, x):
    return dot_pairs((table[0], table[1]), halves(x), NN)


def split_table(x):
    high = x.astype(jnp.bfloat16)
    low = (x - high.astype(np.float32)).astype(jnp.bfloat16)
    return np.stack([high, low])


NN = ((1,), (0,))
NT = ((1,), (1,))
TN = ((0,), (0,))


def cdf(v):
    return 0.5 + 0.5 * lax.erf(v * HALF_ROOT)


def density(v):
    return DENSITY * jnp.exp(-0.5 * v * v)


def normalise(v):
    average = jnp.mean(v, axis=-1, keepdims=True)
    centred = v - average
    spread = jnp.mean(centred * centred, axis=-1, keepdims=True)
    scale = lax.rsqrt(spread + EPS)
    return centred * scale, scale


def normal_back(unit, scale, weighted):
    m0 = jnp.mean(weighted, axis=-1, keepdims=True)
    m1 = jnp.mean(weighted * unit, axis=-1, keepdims=True)
    return scale * (weighted - m0 - unit * m1)


def call(body, grid, in_specs, out_specs, out_shape, flops, moved, name, scratch=()):
    many = isinstance(out_shape, (list, tuple))
    shapes = list(out_shape) if many else [out_shape]
    vout = VOUT.get(name, ())
    kinds = [pltpu.VMEM if n in vout else pltpu.HBM for n in range(len(shapes))]
    shapes = [k(s.shape, s.dtype) for k, s in zip(kinds, shapes)]
    if name in ('contract0', 'add_leaving', 'final'):
        flops, moved = flops * 10, moved * 10
    run = pl.pallas_call(
        body,
        grid=grid,
        in_specs=in_specs,
        out_specs=out_specs,
        out_shape=shapes if many else shapes[0],
        scratch_shapes=list(scratch),
        name=name,
        cost_estimate=pl.CostEstimate(
            flops=int(flops),
            transcendentals=0,
            bytes_accessed=int(moved),
        ),
        compiler_params=pltpu.CompilerParams(vmem_limit_bytes=LIMIT),
    )

    def go(*operands):
        operands = [
            o
            if o.size <= 8192
            else pltpu.with_memory_space_constraint(
                o, pltpu.VMEM if id(o) in HELD_NOW else pltpu.HBM
            )
            for o in operands
        ]
        outs = run(*operands)
        for n, o in enumerate(outs if many else [outs]):
            if n in vout:
                hold(o)
        return outs

    return go


VOUT = {"spatial": (1,), "feed_forward0": (4,), "feed_forward1": (4,)}


def whole(shape):
    return pl.BlockSpec(shape, lambda *_: (0,) * len(shape))


def build(row_parts, item_parts):
    row_bits = row_parts.bit_length() - 1
    item_bits = item_parts.bit_length() - 1
    device_total = row_parts * item_parts
    lanes = 128

    def flip(x, bit):
        pairs = [(f, f ^ (1 << bit)) for f in range(device_total)]
        return lax.ppermute(x, AXES, pairs)

    def flip_mask(x, mask):
        pairs = [(f, f ^ mask) for f in range(device_total)]
        return lax.ppermute(x, AXES, pairs)

    core_bit = item_bits
    depth_bits = [item_bits + row_bits - 1, item_bits + row_bits - 2]
    plane_a = [item_bits + b for b in range(row_bits - 3, 0, -1)] + list(range(item_bits))
    plane_b = plane_a[::-1]
    low_bits = row_bits - 3 + item_bits
    mixing_low = list(range(low_bits))[::-1]
    masks_a, masks_b = [0], [0]
    for bit_a, bit_b in zip(plane_a, plane_b):
        masks_a = masks_a + [m | (1 << bit_a) for m in masks_a]
        masks_b = masks_b + [m | (1 << bit_b) for m in masks_b]
    place_a = [masks_a.index(m) for m in masks_b]

    def gather_stages(x, bits):
        for bit in bits:
            x = jnp.concatenate([x, flip(x, bit)], axis=0)
        return x

    def scatter_stages(x, bits, axis=0):
        for bit in bits[::-1]:
            stay, leave = jnp.split(x, 2, axis=axis)
            x = stay + flip(leave, bit)
        return x

    def mixing_order(x, index):
        for bit in range(x.shape[0].bit_length() - 1):
            lead = x.reshape((-1, 2, 1 << bit) + x.shape[1:])
            swapped = (index >> bit) % 2 == 1
            x = jnp.where(swapped, lead[:, ::-1], lead).reshape(x.shape)
        return x

    def total(x):
        orders = {
            0: ([core_bit], plane_a, depth_bits),
            1: (depth_bits, [core_bit], plane_a),
            2: ([core_bit], depth_bits, plane_a),
        }[1]
        for bits in orders:
            masks = [0]
            for bit in bits:
                masks = masks + [m | (1 << bit) for m in masks]
            parts = [x] + [flip_mask(x, m) for m in masks[1:]]
            if bits is orders[-1]:
                return parts
            while len(parts) > 1:
                parts = [a + b for a, b in zip(parts[::2], parts[1::2])]
            x = parts[0]

    def local(
        frames,
        counts,
        time_weight,
        first_gain,
        first_shift,
        mixing_weight,
        mixing_bias,
        second_gain,
        second_shift,
        expand_weight,
        expand_bias,
        contract_weight,
        contract_bias,
        output_cotangent,
    ):
        HELD_NOW.clear()
        items, frame_total, rows_local, width, channels = frames.shape
        grid_size = rows_local * row_parts
        tokens = rows_local * width
        wave_rows = MODES * 2 * rows_local
        groups = row_parts // PAIRS
        kept = MODES // groups
        part = kept * 2 * rows_local
        stack = 2 * rows_local
        mode_rows = kept * MODES
        shard = contract_weight.shape[0]
        hidden_total = expand_bias.shape[0]
        hidden_local = hidden_total // 2
        piece_total = len(masks_a)
        half = hidden_local // 2
        unit = half // piece_total
        quarter = half // 2
        block_size = channels // BLOCKS
        aligned = stack % 8 == 0
        tables = make_tables(grid_size, rows_local, row_parts)
        wave_fwd, wave_fwd_t, wave_inv, wave_inv_t, col, col_t = tables
        wave_fwd_t, wave_inv, wave_inv_t = map(split_table, (wave_fwd_t, wave_inv, wave_inv_t))
        col_half, col_t_half = split_table(col), split_table(col_t)

        row_index = lax.axis_index("rows")
        flat = row_index * item_parts + lax.axis_index("items")
        pair = (row_index // (row_parts // 8)) % PAIRS
        top = row_index // (row_parts // 2)
        mixing_index = top * (1 << low_bits) + flat % (1 << low_bits)
        mixing_count = 2 << low_bits

        state = []

        def seq(x):
            return after(x, *state) if state else x

        def done(x):
            state[:] = [x]

        carried = jnp.concatenate([expand_weight.T, contract_weight, mixing_weight], axis=1)
        arrived = flip(carried, depth_bits[0])
        beside = flip(carried, depth_bits[1])
        both_near = jnp.concatenate([carried[:, : 2 * channels], beside[:, : 2 * channels]], axis=0)
        pieces = jnp.stack([mixing_weight, arrived[:, 2 * channels :]])
        pieces = pieces.reshape(2, -1, lanes)
        pieces = gather_stages(pieces, mixing_low)
        axes_total = low_bits + 1

        def turn_axes(x):
            lead = x.reshape((2,) * axes_total + x.shape[1:])
            order = tuple(range(axes_total))[::-1]
            return lead.transpose(order + (axes_total, axes_total + 1)).reshape(x.shape)

        layers = mixing_order(turn_axes(pieces), mixing_index)
        layers = layers.reshape(2, 2, 2, block_size, block_size)

        def blocks_of(w):
            zero = jnp.zeros_like(w[0])
            return jnp.concatenate(
                [jnp.concatenate([w[0], zero], 1), jnp.concatenate([zero, w[1]], 1)], 0
            )

        def big(w):
            real, imag = blocks_of(w[:, 0]), blocks_of(w[:, 1])
            return jnp.concatenate(
                [jnp.concatenate([real, imag], 1), jnp.concatenate([-imag, real], 1)], 0
            )

        mix_weight = [big(layers[0]), big(layers[1])]
        bias_pairs = mixing_bias.reshape(2, 2, PAIRS, lanes)
        mix_bias = lax.dynamic_index_in_dim(bias_pairs, pair, 2, keepdims=False)
        mix_bias = mix_bias.reshape(2, 1, 2 * lanes)

        first_bit, second_bit = (1 << b for b in depth_bits)
        masks = [
            far | p | near for far in (0, first_bit) for p in masks_a for near in (0, second_bit)
        ]
        owners = flat ^ jnp.array(masks, dtype=jnp.int32)
        pick = (
            owners[:, None] == jnp.arange(device_total, dtype=jnp.int32)[None, :]
        ).astype(F32)
        bias_shards = expand_bias.reshape(device_total, shard)
        bias_local = jnp.dot(pick, bias_shards, precision=HIGHEST).reshape(1, hidden_local)

        as_row = lambda x: x.reshape(1, channels)
        gain_one, shift_one = as_row(first_gain), as_row(first_shift)
        gain_two, shift_two = as_row(second_gain), as_row(second_shift)

        def put_parts(ref, values):
            if not aligned:
                ref[0] = values
                return
            for g in range(groups):
                for p in range(PAIRS):
                    ref[g // (groups // 2), p, g % (groups // 2), 0] = values[
                        g * part : (g + 1) * part, p * lanes : (p + 1) * lanes
                    ]

        def get_parts(ref):
            if not aligned:
                return ref[0]
            rows = []
            for g in range(groups):
                rows.append(
                    jnp.concatenate(
                        [
                            ref[g // (groups // 2), p, g % (groups // 2), 0]
                            for p in range(PAIRS)
                        ],
                        axis=1,
                    )
                )
            return jnp.concatenate(rows, axis=0)

        def parts_type(count):
            shape = (2, PAIRS, groups // 2, count, part, lanes)
            if not aligned:
                shape = (count, wave_rows, channels)
            return jax.ShapeDtypeStruct(shape, F32)

        if aligned:
            parts_spec = pl.BlockSpec(
                (2, PAIRS, groups // 2, 1, part, lanes), lambda i: (0, 0, 0, i, 0, 0)
            )
        else:
            parts_spec = pl.BlockSpec((1, wave_rows, channels), lambda i: (i, 0, 0))

        def to_send(x, count):
            if aligned:
                return x
            x = x.reshape(count, 2, groups // 2, part, PAIRS, lanes)
            return x.transpose(1, 4, 2, 0, 3, 5)

        def from_send(x, count):
            x = x.reshape(2, PAIRS, groups // 2, count, part, lanes)
            if aligned:
                return x
            return x.transpose(3, 0, 2, 4, 1, 5).reshape(count, wave_rows, channels)

        def exchange(x):
            return lax.all_to_all(x.reshape(row_parts, -1, lanes), "rows", 0, 0)

        def column_type(count):
            shape = (row_parts, count, kept, stack, lanes)
            if not aligned:
                shape = (count, kept, row_parts * stack, lanes)
            return jax.ShapeDtypeStruct(shape, F32)

        if aligned:
            column_spec = pl.BlockSpec(
                (row_parts, 1, kept, stack, lanes), lambda i: (0, i, 0, 0, 0)
            )
        else:
            column_spec = pl.BlockSpec(
                (1, kept, row_parts * stack, lanes), lambda i: (i, 0, 0, 0)
            )

        def to_columns(x, count):
            x = x.reshape(row_parts, count, kept, stack, lanes)
            if aligned:
                return x
            return x.transpose(1, 2, 0, 3, 4).reshape(column_type(count).shape)

        def from_columns(x, count):
            if aligned:
                return x
            x = x.reshape(count, kept, row_parts, stack, lanes)
            return x.transpose(2, 0, 1, 3, 4)

        def get_columns(ref):
            if aligned:
                pieces = [ref[:, 0, k].reshape(row_parts * stack, lanes) for k in range(kept)]
            else:
                pieces = [ref[0, k] for k in range(kept)]
            return jnp.concatenate(pieces, axis=1)

        def put_columns(ref, values):
            for k in range(kept):
                piece = values[:, k * lanes : (k + 1) * lanes]
                if aligned:
                    ref[:, 0, k] = piece.reshape(row_parts, stack, lanes)
                else:
                    ref[0, k] = piece

        def modes_rows(m):
            cut = lambda p, k: m[p * MODES : (p + 1) * MODES, k * lanes : (k + 1) * lanes]
            return jnp.concatenate(
                [jnp.concatenate([cut(0, k), cut(1, k)], axis=1) for k in range(kept)], axis=0
            )

        def rows_modes(z):
            cut = lambda p, k: z[k * MODES : (k + 1) * MODES, p * lanes : (p + 1) * lanes]
            return jnp.concatenate(
                [jnp.concatenate([cut(0, k), cut(1, k)], axis=0) for k in range(kept)], axis=1
            )

        def live_row(counts_ref, item, f):
            seen = jnp.full((1, channels), counts_ref[item], jnp.int32)
            return jnp.where(seen > f, 1.0 / seen.astype(F32), 0.0)

        item_spec = pl.BlockSpec((1, tokens, channels), lambda i: (i, 0, 0))
        item_type = jax.ShapeDtypeStruct((items, tokens, channels), F32)
        frames_spec = pl.BlockSpec(
            (1, frame_total, rows_local, width, channels), lambda i: (i, 0, 0, 0, 0)
        )
        time_spec = whole((frame_total, channels))
        counts_spec = pl.BlockSpec(memory_space=pltpu.SMEM)
        row_spec = whole((1, channels))
        slab_bytes = tokens * channels * 4
        wave_flops = 2 * wave_rows * tokens * channels

        def head_body(counts_ref, frames_ref, time_ref, gain_ref, shift_ref, table_ref, merged_ref, parts_ref):
            item = pl.program_id(0)
            merged = 0.0
            for f in range(frame_total):
                frame = frames_ref[0, f].reshape(tokens, channels)
                merged = merged + frame * (live_row(counts_ref, item, f) * time_ref[f : f + 1, :])
            merged_ref[0] = merged
            unit, _ = normalise(merged)
            normed = unit * gain_ref[...] + shift_ref[...]
            put_parts(parts_ref, dot_full(table_ref[...], normed))

        merged, head_parts = call(
            head_body,
            (items,),
            [counts_spec, frames_spec, time_spec, row_spec, row_spec, whole(wave_fwd.shape)],
            [item_spec, parts_spec],
            [item_type, parts_type(items)],
            6 * items * wave_flops,
            items * slab_bytes * (frame_total + 2),
            "head",
        )(counts, frames, time_weight, gain_one, shift_one, wave_fwd)
        done(merged)
        columns = hold(to_columns(exchange(to_send(head_parts, items)), items))

        far = arrived[:, : 2 * channels]
        batches = [seq(both_near), jnp.concatenate([far, flip(seq(far), depth_bits[1])], axis=0)]

        def gather_plane(x):
            got = {0: x}
            for bit in plane_a:
                for m in list(got):
                    got[m | (1 << bit)] = flip(got[m], bit)
            return [got[m] for m in masks_a]

        shards = [gather_plane(batches[0])]

        cot_own = output_cotangent.reshape(items * tokens, channels)
        cot_other = hold(flip(cot_own, core_bit))
        token_total = items * tokens
        block = tokens
        token_spec = pl.BlockSpec((block, channels), lambda i: (i, 0))
        half_flops = 2 * 3 * token_total * channels * half
        count = piece_total // 2
        up_spec = pl.BlockSpec((unit, channels), lambda *_: (0, 0))
        down_spec = pl.BlockSpec((unit, channels), lambda *_: (0, 1))
        scratch_one = [pltpu.VMEM((half, channels), BF16)] * 2
        scratch_two = [pltpu.VMEM((hidden_local, channels), BF16)] * 2

        def split_into(refs, high_ref, low_ref):
            @pl.when(pl.program_id(0) == 0)
            def _():
                for n, r in enumerate(refs):
                    cut = slice(n * unit, (n + 1) * unit)
                    high_ref[cut, :], low_ref[cut, :] = halves(r[...])

        def cot_body(g1_ref, g2_ref, *refs):
            w_refs, outs, (wh, wl) = refs[:piece_total], refs[piece_total:-2], refs[-2:]
            split_into(w_refs, wh, wl)
            w = (wh[...], wl[...])
            g1, g2 = halves(g1_ref[...]), halves(g2_ref[...])
            outs[0][...] = dot_pairs(g1, w, NT)
            outs[1][...] = dot_pairs(g2, w, NT)
            if len(outs) > 2:
                outs[2][...], outs[3][...] = g1
                outs[4][...], outs[5][...] = g2

        def cot_call(w, extra):
            spec = pl.BlockSpec((block, half), lambda i: (i, 0))
            kind = jax.ShapeDtypeStruct((token_total, half), F32)
            slim_kind = jax.ShapeDtypeStruct((token_total, channels), BF16)
            out = call(
                cot_body,
                (items,),
                [token_spec, token_spec] + [down_spec] * piece_total,
                [spec, spec] + [token_spec] * extra,
                [kind, kind] + [slim_kind] * extra,
                2 * half_flops,
                token_total * (half + channels) * 8,
                "cotangent_up",
                scratch_one,
            )(cot_own, cot_other, seq(w[0]), *w[1:])
            done(out[0])
            return out

        mode_spec = pl.BlockSpec((mode_rows, 2 * lanes), lambda i: (i, 0))
        mode_type = jax.ShapeDtypeStruct((items * mode_rows, 2 * lanes), F32)
        square = (2 * lanes, 2 * lanes)
        weight_spec = whole(square)
        bias_spec = whole((2, 1, 2 * lanes))
        mix_flops = 2 * items * (2 * mode_rows * 4 * lanes * lanes + 2 * col.size * kept * lanes)

        def layer(z, w):
            zr, zi = z[:, :lanes], z[:, lanes:]
            real = dot_full(zr, w[:lanes, :lanes]) + dot_full(zi, w[lanes:, :lanes])
            imag = dot_full(zi, w[lanes:, lanes:]) + dot_full(zr, w[:lanes, lanes:])
            return jnp.concatenate([real, imag], axis=1)

        same = (np.arange(2 * MODES) // MODES)[:, None] == (
            np.arange(col.shape[1]) // rows_local % 2
        )[None, :]
        col_two = np.stack([np.where(same, col, 0), np.where(same, 0, col)]).astype(np.float32)

        def mix_body(x_ref, w0_ref, w1_ref, b_ref, col_ref, col_t_ref, out_ref, z_ref, u_ref, v_ref):
            x = get_columns(x_ref)
            z = modes_rows(dot_full(col_ref[0], x) + dot_full(col_ref[1], x))
            z_ref[...] = z
            u = layer(z, w0_ref[...]) + b_ref[0]
            u_ref[...] = u
            v = layer(u * cdf(u), w1_ref[...]) + b_ref[1]
            v_ref[...] = v
            mixed = v - jnp.clip(v, -SHRINK, SHRINK)
            put_columns(out_ref, dot_split(col_t_ref[...], rows_modes(mixed)))

        first_gates = [batches[1]] if 1 else []
        if 2 == 1:
            first_gates += shards[0][1:]
        if 2 == 2:
            first_gates += [s for m, s in zip(masks_a, shards[0]) if m in [1 << b for b in plane_a]]
        if 0 == 0:
            shards.append(gather_plane(batches[1]))
        mixed = call(
            mix_body,
            (items,),
            [column_spec, weight_spec, weight_spec, bias_spec]
            + [whole(col_two.shape), whole(col_t_half.shape)],
            [column_spec, mode_spec, mode_spec, mode_spec],
            [column_type(items), mode_type, mode_type, mode_type],
            6 * mix_flops,
            items * slab_bytes * 4,
            "mix",
        )(after(seq(columns), *first_gates), *mix_weight, mix_bias, col_two, col_t_half)
        done(mixed[1])
        single = [1 << b for b in plane_a]
        near = [s for m, s in zip(masks_a, shards[1]) if m in single]
        rest = [s for m, s in zip(masks_a, shards[0]) if m and m not in single]
        a1 = {0: [], 1: near + rest, 2: near, 3: near[:1], 4: near[:1] + rest}[4]
        row_back = hold(from_send(exchange(after(from_columns(mixed[0], items), *a1)), items))

        def spatial_body(parts_ref, merged_ref, gain_ref, shift_ref, table_ref, middle_ref, normed_ref):
            middle = merged_ref[0] + dot_split(table_ref[...], get_parts(parts_ref))
            middle_ref[0] = middle
            unit, _ = normalise(middle)
            normed_ref[0] = unit * gain_ref[...] + shift_ref[...]

        def spatial_call(parts, *gates):
            out = call(
                spatial_body,
                (items,),
                [parts_spec, item_spec, row_spec, row_spec, whole(wave_inv.shape)],
                [item_spec, item_spec],
                [item_type, item_type],
                3 * items * wave_flops,
                items * slab_bytes * 4,
                "spatial",
            )(after(seq(parts), *gates), merged, gain_two, shift_two, wave_inv)
            done(out[0])
            return out

        wide = (token_total, hidden_local)
        wide_half = jax.ShapeDtypeStruct(wide, BF16)
        slim_half = jax.ShapeDtypeStruct((token_total, channels), BF16)
        wide_spec = pl.BlockSpec((tokens, hidden_local), lambda i: (i, 0))

        def feed_body(n_ref, bias_ref, ga_ref, gb_ref, *refs):
            w_refs = refs[: 2 * piece_total]
            hh, hl, ph, pl_, grad_ref, bg_ref, nh, nl, wh_ref, wl_ref = refs[2 * piece_total :]
            split_into(w_refs, wh_ref, wl_ref)

            @pl.when(pl.program_id(0) == 0)
            def _():
                bg_ref[...] = jnp.zeros_like(bg_ref)

            n = halves(n_ref[0])
            nh[...], nl[...] = n
            grad = 0.0
            for q in range(4):
                cut = slice(q * quarter, (q + 1) * quarter)
                w = (wh_ref[cut, :], wl_ref[cut, :])
                g_cut = slice(q % 2 * quarter, (q % 2 + 1) * quarter)
                raised = (ga_ref, gb_ref)[q // 2][:, g_cut]
                pre = dot_pairs(n, w, NT) + bias_ref[:, cut]
                phi = cdf(pre)
                hh[:, cut], hl[:, cut] = halves(pre * phi)
                gp = raised * (phi + pre * density(pre))
                bg_ref[:, cut] += jnp.sum(gp, axis=0, keepdims=True)
                gp = halves(gp)
                ph[:, cut], pl_[:, cut] = gp
                grad = grad + dot_pairs(gp, w, NN)
            grad_ref[0] = grad

        def feed_call(side, n):
            out = call(
                feed_body,
                (items,),
                [item_spec, whole((1, hidden_local))]
                + [pl.BlockSpec((tokens, half), lambda i: (i, 0))] * 2
                + [up_spec] * (2 * piece_total),
                [wide_spec] * 4
                + [item_spec, whole((1, hidden_local))]
                + [token_spec] * 2,
                [wide_half] * 4
                + [item_type, jax.ShapeDtypeStruct((1, hidden_local), F32)]
                + [slim_half] * 2,
                2 * 2 * 3 * token_total * channels * hidden_local,
                token_total * (hidden_local * 3 + channels * 3) * 4,
                f"feed_forward{side}",
                scratch_two,
            )(seq(n), bias_local, raised[0][side], raised[1][side], *shards[0], *shards[1])
            done(out[4])
            return out

        def middle_body(
            mid_ref, g1_ref, g2_ref, cot_ref, gain_ref, table_ref, gm_ref, parts_ref, small_ref
        ):
            unit, scale = normalise(mid_ref[0])
            grad = g1_ref[0] + g2_ref[0]
            cot = cot_ref[...]
            gm = cot + normal_back(unit, scale, grad * gain_ref[...])
            gm_ref[0] = gm
            put_parts(parts_ref, dot_split(table_ref[...], gm))

            @pl.when(pl.program_id(0) == 0)
            def _():
                small_ref[...] = jnp.zeros_like(small_ref)

            small_ref[0:1, :] += jnp.sum(grad * unit, axis=0, keepdims=True)
            small_ref[1:2, :] += jnp.sum(grad, axis=0, keepdims=True)
            small_ref[2:3, :] += jnp.sum(cot, axis=0, keepdims=True)

        small_type = jax.ShapeDtypeStruct((8, channels), F32)
        small_spec = whole((8, channels))

        if 0 == 1:
            shards.append(gather_plane(after(batches[1], mixed[1])))
        raised = [cot_call(shards[0], 4)]
        if not 0:
            raised.append(cot_call(shards[1], 0))
        middle, normed_own = spatial_call(row_back)
        normed_other = hold(flip(normed_own, core_bit))
        if 0:
            raised.append(cot_call(shards[1], 0))
        fed = [feed_call(0, normed_own), feed_call(1, normed_other)]
        grad_middle, middle_parts, small_two = call(
            middle_body,
            (items,),
            [item_spec] * 3 + [token_spec, row_spec, whole(wave_inv_t.shape)],
            [item_spec, parts_spec, small_spec],
            [item_type, parts_type(items), small_type],
            3 * items * wave_flops,
            items * slab_bytes * 6,
            "middle_back",
        )(middle, fed[0][4], seq(hold(flip(fed[1][4], core_bit))), cot_own, gain_two, wave_inv_t)
        done(small_two)
        grad_columns = hold(to_columns(exchange(to_send(middle_parts, items)), items))

        lane_block = unit % lanes == 0
        wide_count = count if lane_block else 1

        def outer_body(*refs):
            outs = refs[-4:] if refs[-1].ndim == 3 else refs[-2:]
            contract_out, expand_out = 0.0, 0.0
            per_side = 2 * wide_count + 6
            for s in range(2):
                mine = refs[per_side * s : per_side * (s + 1)]
                h = tuple(
                    jnp.concatenate(
                        [r[...] for r in mine[n * wide_count : (n + 1) * wide_count]], axis=1
                    )
                    for n in range(2)
                )
                ph, pl_, gh, gl, nh, nl = [r[...] for r in mine[2 * wide_count :]]
                contract_out += dot_pairs(h, (gh, gl), TN)
                expand_out += dot_pairs((ph, pl_), (nh, nl), TN)
            if len(outs) == 4:
                for o, x in ((0, contract_out), (2, expand_out)):
                    for side in range(2):
                        for b in range(outs[0].shape[0]):
                            at = (b * 2 + side) * outs[0].shape[1]
                            outs[o + side][b] = x[at : at + outs[0].shape[1], :]
            else:
                outs[0][...], outs[1][...] = contract_out, expand_out

        def outer_call(side):
            picks = place_a[side * count : (side + 1) * count]

            def unit_spec(p):
                return pl.BlockSpec((token_total, unit), lambda b: (0, b * piece_total + p))

            def gathered(x):
                return jnp.concatenate(
                    [
                        x[:, b * half + p * unit : b * half + (p + 1) * unit]
                        for b in range(2)
                        for p in picks
                    ],
                    axis=1,
                )

            def half_of(x):
                return jnp.concatenate(
                    [x[:, b * half + side * quarter :][:, :quarter] for b in range(2)], axis=1
                )

            specs, operands = [], []
            slim_spec = whole((token_total, channels))
            for s in range(2):
                values = fed[s]
                if lane_block:
                    specs += [unit_spec(p) for p in picks] * 2
                    specs += [
                        pl.BlockSpec((token_total, quarter), lambda b: (0, b * 2 + side))
                    ] * 2
                    operands += [values[0]] * count + [values[1]] * count + list(values[2:4])
                else:
                    specs += [whole((token_total, half))] * 4
                    operands += [gathered(v) for v in values[:2]]
                    operands += [half_of(v) for v in values[2:4]]
                specs += [slim_spec] * 4
                operands += list(raised[0][2 + 2 * s : 4 + 2 * s]) + list(values[6:8])
            operands[0] = seq(operands[0])
            rows = quarter if lane_block else half
            row_block = pl.BlockSpec((rows, channels), lambda b: (b, 0))
            if side == 0:
                eighth = quarter // 2
                outs = [jax.ShapeDtypeStruct((2, eighth, channels), F32)] * 4
                batches_here = rows // quarter
                out_specs = [
                    pl.BlockSpec((batches_here, eighth, channels), lambda b: (b, 0, 0))
                ] * 4
            else:
                outs = [jax.ShapeDtypeStruct((half, channels), F32)] * 2
                out_specs = [row_block] * 2
            out = call(
                outer_body,
                (half // rows,),
                specs,
                out_specs,
                outs,
                4 * half_flops,
                token_total * (half + channels) * 16,
                f"weight_grads{side}",
            )(*operands)
            done(out[0])
            return out

        leaving = outer_call(1)
        staying = outer_call(0) if 1 else None
        contract_there = hold(flip(leaving[0], plane_b[-1]))
        expand_there = hold(flip(leaving[1], plane_a[-1]))

        def contract_calls():
            def down_body(hh, hl, *refs):
                extra = refs[: -3 - 2 * piece_total]
                w_refs, (out_ref, wh_ref, wl_ref) = refs[-3 - 2 * piece_total : -3], refs[-3:]
                split_into(w_refs, wh_ref, wl_ref)
                out = dot_pairs((hh[...], hl[...]), (wh_ref[...], wl_ref[...]), NN)
                if extra:
                    out = out + extra[0][0] + extra[1][0] + extra[2][...]
                out_ref[0] = out

            def down_call(side, extra, specs):
                out = call(
                    down_body,
                    (items,),
                    [wide_spec] * 2 + specs + [down_spec] * (2 * piece_total),
                    item_spec,
                    item_type,
                    2 * 3 * token_total * channels * hidden_local,
                    token_total * (hidden_local + channels) * 4,
                    f"contract{side}",
                    scratch_two,
                )(seq(fed[side][0]), fed[side][1], *extra, *shards[0], *shards[1])
                done(out)
                return out

            return down_call

        down_call = contract_calls()

        def finish_output(there):
            extra = [middle, there, as_row(contract_bias)]
            return down_call(0, extra, [item_spec, item_spec, row_spec])

        if 4 in (1, 2, 3):
            there = hold(flip(down_call(1, [], []), core_bit))
        if 4 == 1:
            block_out = finish_output(there)

        def mix_back_body(
            x_ref, z_ref, u_ref, v_ref, w0_ref, w1_ref, col_ref, col_t_ref, out_ref, wg_ref, bg_ref, sum_ref
        ):
            step = pl.program_id(0)
            grad = modes_rows(dot_split(col_ref[...], get_columns(x_ref)))
            e1 = jnp.where(jnp.abs(v_ref[...]) > SHRINK, grad, 0.0)
            u = u_ref[...]
            phi = cdf(u)
            e1_half = halves(e1)
            e0 = dot_pairs(e1_half, halves(w1_ref[...]), NT) * (phi + u * density(u))
            e0_half = halves(e0)
            dz = dot_pairs(e0_half, halves(w0_ref[...]), NT)
            put_columns(out_ref, dot_split(col_t_ref[...], rows_modes(dz)))

            @pl.when(step == 0)
            def _():
                sum_ref[...] = jnp.zeros_like(sum_ref)
                bg_ref[...] = jnp.zeros_like(bg_ref)

            sum_ref[0] += dot_pairs(halves(z_ref[...]), e0_half, TN)
            sum_ref[1] += dot_pairs(halves(u * phi), e1_half, TN)
            bg_ref[0] += jnp.sum(e0, axis=0, keepdims=True)
            bg_ref[1] += jnp.sum(e1, axis=0, keepdims=True)

            @pl.when(step == items - 1)
            def _():
                for layer in range(2):
                    w = sum_ref[layer]
                    real = w[:lanes, :lanes] + w[lanes:, lanes:]
                    imag = w[:lanes, lanes:] - w[lanes:, :lanes]
                    for b in range(2):
                        cut = slice(b * block_size, (b + 1) * block_size)
                        wg_ref[layer, b, 0] = real[cut, cut]
                        wg_ref[layer, b, 1] = imag[cut, cut]

        grad_shape = (2, 2, 2, block_size, block_size)
        back_parts, mix_grad, big_bias = call(
            mix_back_body,
            (items,),
            [column_spec, mode_spec, mode_spec, mode_spec, weight_spec, weight_spec]
            + [whole(col_half.shape), whole(col_t_half.shape)],
            [column_spec, whole(grad_shape), bias_spec],
            [
                column_type(items),
                jax.ShapeDtypeStruct(grad_shape, F32),
                jax.ShapeDtypeStruct((2, 1, 2 * lanes), F32),
            ],
            3 * 2 * mix_flops,
            items * slab_bytes * 4,
            "mix_back",
            [pltpu.VMEM((2,) + square, F32)],
        )(seq(grad_columns), *mixed[1:], *mix_weight, col_half, col_t_half)
        done(big_bias)
        last_parts = hold(from_send(exchange(from_columns(back_parts, items)), items))
        if 4 == 2:
            block_out = finish_output(there)
        if staying is None:
            staying = outer_call(0)
        came = [x.reshape(2, quarter, channels) for x in (contract_there, expand_there)]
        if 4 == 4:
            there = hold(flip(down_call(1, [], []), core_bit))

        def add_body(a_ref, b_ref, c_ref, d_ref, o1_ref, o2_ref):
            o1_ref[...] = a_ref[...] + b_ref[...]
            o2_ref[...] = c_ref[...] + d_ref[...]

        thin = (1, quarter // 2, channels)
        first_part = pl.BlockSpec(thin, lambda b: (b, 0, 0))
        second_part = pl.BlockSpec(thin, lambda b: (b, 1, 0))
        leave_kind = jax.ShapeDtypeStruct((2, quarter // 2, channels), F32)
        leave_c, leave_e = call(
            add_body,
            (2,),
            [first_part, second_part] * 2,
            [first_part] * 2,
            [leave_kind] * 2,
            0,
            half * channels * 12,
            "add_leaving",
        )(seq(staying[1]), came[0], staying[3], came[1])
        done(leave_c)
        if 4 == 3:
            block_out = finish_output(there)
        if 4 == 4 and 1:
            block_out = finish_output(there)
        mix_grad = mix_grad.reshape(mixing_count, -1, lanes)
        mix_grad = turn_axes(mixing_order(mix_grad, mixing_index))
        mix_stay, mix_leave = jnp.split(mix_grad, 2, axis=0)
        travelling = []
        for stay, leave, got, bits in (
            (staying[2], leave_e, came[1], plane_a),
            (staying[0], leave_c, came[0], plane_b),
        ):
            stay = stay + got[:, : quarter // 2]
            for bit in bits[1:-1][::-1]:
                stay, leave = jnp.split(stay + flip(leave, bit), 2, axis=1)
            if bits[0] == mixing_low[-1]:
                rows_two = [leave.reshape(-1, channels), mix_leave.reshape(-1, channels)]
                leave = jnp.concatenate(rows_two, axis=0)
            travelling.append((stay, flip(leave, bits[0])))
        if 4 == 0:
            block_out = finish_output(hold(flip(down_call(1, [], []), core_bit)))

        def final_body(
            counts_ref,
            parts_ref,
            merged_ref,
            *refs,
        ):
            gm_ref, frames_ref, gain_ref, table_ref, total_ref, small_ref = refs
            item = pl.program_id(0)
            grad = dot_split(table_ref[...], get_parts(parts_ref))
            unit, scale = normalise(merged_ref[0])
            gm = gm_ref[0] + normal_back(unit, scale, grad * gain_ref[...])
            total_ref[0] = gm

            @pl.when(item == 0)
            def _():
                small_ref[...] = jnp.zeros_like(small_ref)

            small_ref[frame_total : frame_total + 1, :] += jnp.sum(
                grad * unit, axis=0, keepdims=True
            )
            small_ref[frame_total + 1 : frame_total + 2, :] += jnp.sum(
                grad, axis=0, keepdims=True
            )
            for f in range(frame_total):
                live = live_row(counts_ref, item, f)
                frame = frames_ref[0, f].reshape(tokens, channels)
                small_ref[f : f + 1, :] += live * jnp.sum(frame * gm, axis=0, keepdims=True)

        grad_merged, small_one = call(
            final_body,
            (items,),
            [counts_spec, parts_spec, item_spec, item_spec]
            + [frames_spec, row_spec, whole(wave_fwd_t.shape)],
            [item_spec, small_spec],
            [item_type, small_type],
            3 * items * wave_flops,
            items * slab_bytes * (4 + frame_total),
            "final",
        )(
            counts,
            seq(last_parts),
            merged,
            grad_middle,
            frames,
            gain_one,
            wave_fwd_t,
        )
        done(small_one)

        def frames_body(counts_ref, gm_ref, time_ref, out_ref):
            item = pl.program_id(0)
            gm = gm_ref[0]
            for f in range(frame_total):
                factor = live_row(counts_ref, item, f) * time_ref[f : f + 1, :]
                out_ref[0, f] = (gm * factor).reshape(rows_local, width, channels)

        frames_grad = call(
            frames_body,
            (items,),
            [counts_spec, item_spec, time_spec],
            frames_spec,
            jax.ShapeDtypeStruct(frames.shape, F32),
            0,
            items * slab_bytes * (1 + frame_total),
            "frames_grad",
        )(counts, seq(grad_merged), time_weight)

        if 1:
            gate = small_one if 1 == 1 else block_out
            travelling = [(s, after(r, gate)) for s, r in travelling]
        stays, gots = zip(*travelling)
        span = stays[1].shape[0] * stays[1].shape[1]
        mix_got = gots[1][span:].reshape(mix_stay.shape)
        gots = [gots[0], gots[1][:span].reshape(stays[1].shape)]
        joined = jnp.concatenate([s + r for s, r in zip(stays, gots)], axis=2)
        mix_grad = scatter_stages(mix_stay + mix_got, mixing_low[:-1])
        blocks = joined.reshape(2, 2, shard, 2 * channels)
        leaving_far = jnp.concatenate(
            [blocks[1, 0], mix_grad[1].reshape(-1, 2 * channels)], axis=0
        )
        arrived_last = flip(leaving_far, depth_bits[0])
        got_both = flip_mask(blocks[1, 1], (1 << depth_bits[0]) | (1 << depth_bits[1]))
        got_near = flip(blocks[0, 1], depth_bits[1])
        both_grad = (blocks[0, 0] + got_near) + (arrived_last[:shard] + got_both)
        mixing_weight_grad = mix_grad[0].reshape(mixing_weight.shape) + arrived_last[
            shard:
        ].reshape(mixing_weight.shape)
        expand_weight_grad = both_grad[:, :channels].T
        contract_weight_grad = both_grad[:, channels:]

        bias_grad_local = fed[0][5] + fed[1][5]
        bias_full = jnp.zeros((2, 2, PAIRS, lanes), F32)
        bias_full = lax.dynamic_update_slice(
            bias_full, big_bias.reshape(2, 2, 1, lanes), (0, 0, pair, 0)
        ).reshape(4, channels)
        hidden_bias = jnp.dot(
            pick.T, bias_grad_local.reshape(-1, shard), precision=HIGHEST
        ).reshape(-1, channels)
        at = frame_total
        rows = jnp.concatenate(
            [small_one[: at + 2], small_two[:3], bias_full, hidden_bias], axis=0
        )
        parts = total(rows)
        widths = [at, 1, 1, 1, 1, 1, 4, rows.shape[0] - at - 9]

        def finish_body(*refs):
            ins, outs = refs[: len(parts)], refs[len(parts) :]
            sums = [r[...] for r in ins]
            while len(sums) > 1:
                sums = [a + b for a, b in zip(sums[::2], sums[1::2])]
            row = 0
            for out, count in zip(outs, widths):
                out[...] = sums[0][row : row + count, :]
                row += count

        finals = call(
            finish_body,
            (1,),
            [whole(rows.shape)] * len(parts),
            [whole((w, channels)) for w in widths],
            [jax.ShapeDtypeStruct((w, channels), F32) for w in widths],
            0,
            rows.size * 24,
            "sums",
        )(*parts)
        time_grad, gain_1, shift_1, gain_2, shift_2, bias_c, mix_bias_grad, bias_e = finals

        return (
            block_out.reshape(output_cotangent.shape),
            frames_grad,
            time_grad,
            gain_1.reshape(channels),
            shift_1.reshape(channels),
            mixing_weight_grad,
            mix_bias_grad,
            gain_2.reshape(channels),
            shift_2.reshape(channels),
            expand_weight_grad,
            bias_e.reshape(hidden_total),
            contract_weight_grad,
            bias_c.reshape(channels),
        )

    return local


def solution(mesh):
    return jax.shard_map(
        build(mesh.shape["rows"], mesh.shape["items"]),
        mesh=mesh,
        in_specs=(
            P("items", None, "rows", None, None),
            P("items"),
            P(),
            P(),
            P(),
            P(("rows", "items"), None),
            P(),
            P(),
            P(),
            P(None, ("rows", "items")),
            P(),
            P(("rows", "items"), None),
            P(),
            P("items", "rows", None, None),
        ),
        out_specs=(
            P("items", "rows", None, None),
            P("items", None, "rows", None, None),
            P(),
            P(),
            P(),
            P(("rows", "items"), None),
            P(),
            P(),
            P(),
            P(None, ("rows", "items")),
            P(),
            P(("rows", "items"), None),
            P(),
        ),
        check_vma=False,
    )
```
